32 devices in a mesh: seq: 16 (over z, y, x), mp: 2 (over core).
Axes of the slice: x: 2, y: 2, z: 4, core: 2. Of those that a mesh axis runs over, the one named last changes fastest.
Arguments:
- inner_act: bfloat16 [2048, 6144], P('seq', 'mp'), may hold values from -6 to 6
- gate_act: bfloat16 [2048, 6144], P('seq', 'mp'), may hold values from -6 to 6
- x_proj: bfloat16 [6144, 224], P('mp'), may hold values from -0.078125 to 0.078125
- dt_proj: bfloat16 [192, 6144], P(None, 'mp'), may hold values from -0.4375 to 0.4375
- dt_bias: float32 [6144], P('mp'), may hold values from -5.5 to -3.5
- a_log: float32 [16, 6144], P(None, 'mp'), may hold values from -12 to 2.3
- skip: float32 [6144], P('mp'), may hold values from 0.5 to 1.5
Outputs:
- mixed_out: bfloat16 [2048, 6144], P('seq', 'mp')
The draws below stay inside these ranges and needn't reach their ends.
All inputs are finite; a program needn't handle non-finite values.
Results may differ from the reference program's by a relative error of at most 0.0095.
Values sent between devices are 32-bit elements; how exact they have to be, the bound alone decides.
A program may use at most 128 MiB of HBM per device.

```python
import jax
import jax.numpy as jnp
from jax import lax

INNER = 6144
STATES = 16
DT_RANK = 192
TOKENS = 2048


def level_of(key, dims, pieces, least, largest):
    loudness, own = 1.0, jax.random.fold_in(key, 6)
    for dim, shards_of in pieces:
        heights = jnp.exp(jax.random.uniform(jax.random.fold_in(own, dim), (shards_of,), jnp.float32, least / len(pieces), largest / len(pieces)))
        loudness = loudness * jnp.repeat(heights, dims[dim] // shards_of).reshape([-1 if axis == dim else 1 for axis in range(len(dims))])
    return loudness


def gaussian(key, dims, scale, limit, cuts=(), dtype=jnp.bfloat16):
    level = level_of(key, dims, cuts, -0.22, 0.18) if cuts else 1.0
    entries = jax.random.normal(key, dims, jnp.float32) * scale * level
    return jnp.minimum(jnp.maximum(entries, -limit), limit).astype(dtype)


def setup_inputs(seed: int = 0) -> dict:
    keys = jax.random.split(jax.random.key(seed), 8)
    return {
        "inner_act": gaussian(keys[0], (TOKENS, INNER), 1.0, 6.0, ((0, 16), (1, 2))),
        "gate_act": gaussian(keys[1], (TOKENS, INNER), 1.0, 6.0, ((0, 16), (1, 2))),
        "x_proj": gaussian(keys[2], (INNER, DT_RANK + 2 * STATES), INNER ** -0.5, 0.078125, ((0, 2),)),
        "dt_proj": gaussian(keys[3], (DT_RANK, INNER), DT_RANK ** -0.5, 0.4375, ((1, 2),)),
        "dt_bias": jnp.clip(-5.5 + 2.0 * jax.random.uniform(keys[4], (INNER,), jnp.float32) ** level_of(keys[4], (INNER,), ((0, 2),), -0.2, 0.2), -5.5, -3.5),
        "a_log": jnp.clip(-12.0 + 14.3 * jax.random.uniform(keys[5], (STATES, INNER), jnp.float32) ** level_of(keys[5], (STATES, INNER), ((1, 2),), -0.2, 0.2), -12.0, 2.3),
        "skip": jnp.clip(0.5 + 1.0 * jax.random.uniform(keys[6], (INNER,), jnp.float32) ** level_of(keys[6], (INNER,), ((0, 2),), -0.2, 0.2), 0.5, 1.5),
    }


def recurrence(dt, drive, bmat, cmat, rate, init):
    total = dt.shape[0]
    count = total // 32

    def advance(state, block):
        dt_blk, drive_blk, b_blk, c_blk = block
        outputs = []
        for i in range(32):
            state = jnp.exp(-rate * dt_blk[i][None, :]) * state + b_blk[i][:, None] * drive_blk[i][None, :]
            outputs.append(jnp.sum(c_blk[i][:, None] * state, axis=0))
        return state, jnp.stack(outputs)

    blocks = (dt.reshape(count, 32, -1), drive.reshape(count, 32, -1),
              bmat.reshape(count, 32, -1), cmat.reshape(count, 32, -1))
    final, values = lax.scan(advance, init, blocks)
    return values.reshape(total, -1), final


def reference(inner_act, gate_act, x_proj, dt_proj, dt_bias, a_log, skip):
    proj = jnp.dot(inner_act, x_proj, preferred_element_type=jnp.float32)
    rank = dt_proj.shape[0]
    states = a_log.shape[0]
    low = proj[:, :rank].astype(jnp.bfloat16)
    dt = jax.nn.softplus(jnp.dot(low, dt_proj, preferred_element_type=jnp.float32) + dt_bias[None, :])
    bmat = proj[:, rank:rank + states]
    cmat = proj[:, rank + states:]
    uvalue = inner_act.astype(jnp.float32)
    rate = jnp.exp(a_log)
    ssm, final = recurrence(dt, dt * uvalue, bmat, cmat, rate, jnp.zeros_like(rate))
    mixed = (ssm + skip[None, :] * uvalue) * jax.nn.silu(gate_act.astype(jnp.float32))
    return mixed.astype(jnp.bfloat16)
```

```python
import functools

import jax
import jax.numpy as jnp
from jax import lax
from jax.experimental import pallas as pl
from jax.experimental.pallas import tpu as pltpu
from jax.sharding import PartitionSpec as P

LANES = 128
SUB = 8
TILE = LANES * SUB
UNROLL = 8
LOG2E = 1.4426950408889634
F32 = jnp.float32


def softplus(x):
    e = jnp.exp(-jnp.abs(x))
    series = e * (1.0 - e * (0.5 - e * (1.0 / 3.0 - e * (0.25 - e * 0.2))))
    return jnp.maximum(x, 0.0) + jnp.where(e < 0.03125, series, jnp.log(1.0 + e))


def kernel(seq, mp, tokens, inner, rank, states,
           u_hbm, g_hbm, xp_hbm, dtp_hbm, bias_hbm, alog_hbm, skip_hbm, out_ref,
           u_ref, g_ref, xp_ref, dtp_ref, bias_ref, alog_ref, skip_ref,
           proj, bs, cs, rate, raw, dts, drv, ys, fades, tot, sums, got_e, got_s, back, ent, far, near,
           in_sem, mp_send, mp_recv, e_send, e_recv, s_send, s_recv, b_send, b_recv,
           f_send, f_recv):
    blocks = pl.cdiv(inner, TILE)
    group = states
    groups = seq // group
    me = lax.axis_index("seq")
    my_mp = lax.axis_index("mp")
    mine = lax.rem(me, group)
    my_group = me // group
    base = my_group * group

    loads = [pltpu.make_async_copy(src, dst, in_sem.at[i]) for i, (src, dst) in enumerate((
        (u_hbm, u_ref), (xp_hbm, xp_ref), (alog_hbm, alog_ref), (dtp_hbm, dtp_ref),
        (bias_hbm, bias_ref), (g_hbm, g_ref), (skip_hbm, skip_ref)))]
    for load in loads:
        load.start()

    barrier = pltpu.get_barrier_semaphore()
    for m in range(1, mp):
        pl.semaphore_signal(barrier, inc=1, device_id={"mp": lax.rem(my_mp + m, mp)},
                            device_id_type=pl.DeviceIdType.MESH)
    for p in range(1, group):
        pl.semaphore_signal(barrier, inc=1,
                            device_id={"seq": base + lax.rem(mine + p, group)},
                            device_id_type=pl.DeviceIdType.MESH)
    for p in range(1, groups):
        pl.semaphore_signal(barrier, inc=1, device_id={"seq": lax.rem(me + p * group, seq)},
                            device_id_type=pl.DeviceIdType.MESH)

    loads[0].wait()
    loads[1].wait()
    proj[my_mp] = lax.dot_general(u_ref[...], xp_ref[...], (((1,), (1,)), ((), ())),
                                  preferred_element_type=F32)
    pl.semaphore_wait(barrier, (mp - 1) + (group - 1) + (groups - 1))
    shares = []
    for m in range(1, mp):
        copy = pltpu.make_async_remote_copy(
            src_ref=proj.at[my_mp], dst_ref=proj.at[my_mp],
            send_sem=mp_send.at[m - 1], recv_sem=mp_recv.at[m - 1],
            device_id={"mp": lax.rem(my_mp + m, mp)},
            device_id_type=pl.DeviceIdType.MESH)
        copy.start()
        shares.append(copy)

    loads[2].wait()
    for k in range(blocks):
        for j in range(min(SUB, inner // LANES - k * SUB)):
            lo = (k * SUB + j) * LANES
            rate[k, pl.ds(j, states, stride=SUB), :] = (
                jnp.exp(alog_ref[:, lo:lo + LANES]) * (-LOG2E))
    loads[3].wait()
    loads[4].wait()

    for copy in shares:
        copy.wait()
    whole = proj[0]
    for m in range(1, mp):
        whole = whole + proj[m]
    low = whole[:, :rank].astype(jnp.bfloat16)

    def lanes_of(k):
        return min(SUB, inner // LANES - k * SUB)

    def tile(ref, k, i):
        return ref[k, pl.ds(pl.multiple_of(i * SUB, SUB), SUB), :]

    def steps(k):
        width = lanes_of(k) * LANES
        raw[:, :width] = jnp.dot(low, dtp_ref[:, k * TILE:k * TILE + width],
                                 preferred_element_type=F32)
        @pl.loop(0, lanes_of(k))
        def _(j):
            lo = pl.multiple_of((k * SUB + j) * LANES, LANES)
            cols = pl.ds(lo, LANES)
            dt = softplus(raw[:, pl.ds(pl.multiple_of(j * LANES, LANES), LANES)]
                          + bias_ref[:, cols])
            dts[k, pl.ds(j, tokens, stride=SUB), :] = dt
            drv[k, pl.ds(j, tokens, stride=SUB), :] = dt * u_ref[:, cols].astype(F32)
            sums[k, pl.ds(j, 1), :] = jnp.sum(dt, axis=0, keepdims=True)

        got_s[k, 0] = sums[k]

        @pl.loop(1, group)
        def _(p):
            pltpu.make_async_remote_copy(
                src_ref=sums.at[k], dst_ref=got_s.at[k, group - p],
                send_sem=s_send.at[k], recv_sem=s_recv.at[k],
                device_id={"seq": base + lax.rem(mine + p, group)},
                device_id_type=pl.DeviceIdType.MESH).start()

    def cell(t, n):
        return pl.ds(pl.multiple_of((t * states + n) * SUB, SUB), SUB)

    def ends(k):
        rates = [rate[k, n * SUB:(n + 1) * SUB, :] for n in range(states)]

        def body(it, hs):
            hs = list(hs)
            for i in range(UNROLL):
                t = it * UNROLL + i
                dt = tile(dts, k, t)
                dr = tile(drv, k, t)
                for n in range(states):
                    fade = jnp.exp2(rates[n] * dt)
                    fades[k, cell(t, n), :] = fade
                    hs[n] = fade * hs[n] + bs[n, pl.ds(t, 1), :] * dr
            return tuple(hs)

        zero = jnp.zeros((SUB, LANES), F32)
        final = lax.fori_loop(0, tokens // UNROLL, body, (zero,) * states)
        for n in range(states):
            tot[k, n] = final[n]
        got_e[k, 0] = tot[k, mine]

        @pl.loop(1, group)
        def _(p):
            owner = lax.rem(mine + p, group)
            pltpu.make_async_remote_copy(
                src_ref=tot.at[k, owner], dst_ref=got_e.at[k, group - p],
                send_sem=e_send.at[k], recv_sem=e_recv.at[k],
                device_id={"seq": base + owner},
                device_id_type=pl.DeviceIdType.MESH).start()

    def local(k):
        def body(it, hs):
            hs = list(hs)
            for i in range(UNROLL):
                t = it * UNROLL + i
                dr = tile(drv, k, t)
                acc = [None, None]
                for n in range(states):
                    hs[n] = fades[k, cell(t, n), :] * hs[n] + bs[n, pl.ds(t, 1), :] * dr
                    term = cs[n, pl.ds(t, 1), :] * hs[n]
                    acc[n % 2] = term if acc[n % 2] is None else acc[n % 2] + term
                ys[k, pl.ds(pl.multiple_of(t * SUB, SUB), SUB), :] = acc[0] + acc[1]
            return tuple(hs)

        zero = jnp.zeros((SUB, LANES), F32)
        lax.fori_loop(0, tokens // UNROLL, body, (zero,) * states)

    def drain(ref, k, sem):
        part = ref.at[k, pl.ds(1, group - 1)]
        pltpu.make_async_copy(part, part, sem.at[k]).wait()

    def own(k):
        drain(got_s, k, s_recv)
        drain(got_e, k, e_recv)
        rt = rate[k, pl.ds(pl.multiple_of(mine * SUB, SUB), SUB), :]
        slots = [lax.rem(j - mine + group, group) for j in range(group)]
        carry = jnp.zeros((SUB, LANES), F32)
        if groups > 1:
            end, span = carry, carry
            for slot in slots:
                end = jnp.exp2(rt * got_s[k, slot]) * end + got_e[k, slot]
                span = span + got_s[k, slot]
            near[k, 0] = end
            near[k, 1] = span
            sent = [pltpu.make_async_remote_copy(
                src_ref=near.at[k], dst_ref=far.at[k, groups - p],
                send_sem=f_send.at[k, p], recv_sem=f_recv.at[k, groups - p],
                device_id={"seq": lax.rem(me + p * group, seq)},
                device_id_type=pl.DeviceIdType.MESH) for p in range(1, groups)]
            for copy in sent:
                copy.start()
            for copy in sent:
                copy.wait()
            far[k, 0] = near[k]
            for g in range(groups - 1):
                slot = lax.rem(g - my_group + groups, groups)
                carry = jnp.where(
                    g < my_group, jnp.exp2(rt * far[k, slot, 1]) * carry + far[k, slot, 0], carry)
        for slot in slots:
            back[k, slot] = carry
            carry = jnp.exp2(rt * got_s[k, slot]) * carry + got_e[k, slot]
        ent[k, 0] = back[k, 0]

        @pl.loop(1, group)
        def _(p):
            pltpu.make_async_remote_copy(
                src_ref=back.at[k, p], dst_ref=ent.at[k, group - p],
                send_sem=b_send.at[k], recv_sem=b_recv.at[k],
                device_id={"seq": base + lax.rem(mine + p, group)},
                device_id_type=pl.DeviceIdType.MESH).start()

    def correct(k):
        drain(ent, k, b_recv)
        ents = [ent[k, lax.rem(n - mine + group, group)] for n in range(states)]

        def body(it, es):
            es = list(es)
            for i in range(UNROLL):
                t = it * UNROLL + i
                acc = [tile(ys, k, t), None]
                for n in range(states):
                    es[n] = fades[k, cell(t, n), :] * es[n]
                    term = cs[n, pl.ds(t, 1), :] * es[n]
                    acc[n % 2] = term if acc[n % 2] is None else acc[n % 2] + term
                ys[k, pl.ds(pl.multiple_of(t * SUB, SUB), SUB), :] = acc[0] + acc[1]
            return tuple(es)

        lax.fori_loop(0, tokens // UNROLL, body, tuple(ents))

    def finish(k):
        @pl.loop(0, lanes_of(k))
        def _(j):
            lo = pl.multiple_of((k * SUB + j) * LANES, LANES)
            cols = pl.ds(lo, LANES)
            y = ys[k, pl.ds(j, tokens, stride=SUB), :]
            g = g_ref[:, cols].astype(F32)
            mixed = (y + skip_ref[:, cols] * u_ref[:, cols].astype(F32)) * (
                g / (1.0 + jnp.exp(-g)))
            out_ref[:, cols] = mixed.astype(out_ref.dtype)

    if inner % TILE:
        sums[blocks - 1] = jnp.zeros((SUB, LANES), F32)
    for k in range(blocks):
        steps(k)
    for n in range(states):
        bs[n] = jnp.broadcast_to(whole[:, rank + n:rank + n + 1], (tokens, LANES))
    for k in range(blocks):
        ends(k)
    for n in range(states):
        cs[n] = jnp.broadcast_to(
            whole[:, rank + states + n:rank + states + n + 1], (tokens, LANES))
    for k in range(blocks):
        local(k)
        if k < blocks - 1 or blocks == 1:
            own(k)
        if k == blocks - 2:
            own(blocks - 1)
    loads[5].wait()
    loads[6].wait()
    for k in range(blocks):
        correct(k)
        finish(k)
    for k in range(blocks):
        drain(got_s, k, s_send)
        drain(got_e, k, e_send)
        drain(back, k, b_send)


def solution(mesh):
    seq, mp = mesh.shape["seq"], mesh.shape["mp"]

    def per_device(inner_act, gate_act, x_proj, dt_proj, dt_bias, a_log, skip):
        tokens, inner = inner_act.shape
        rank, states = dt_proj.shape[0], a_log.shape[0]
        blocks = pl.cdiv(inner, TILE)
        group, groups = states, seq // states
        hbm = pl.BlockSpec(memory_space=pltpu.MemorySpace.HBM)
        args = tuple(pltpu.with_memory_space_constraint(a, pltpu.HBM) for a in (
            inner_act, gate_act, x_proj.T, dt_proj, dt_bias.reshape(1, inner), a_log,
            skip.reshape(1, inner)))
        cell = (SUB, LANES)
        dma = pltpu.SemaphoreType.DMA
        return pl.pallas_call(
            functools.partial(kernel, seq, mp, tokens, inner, rank, states),
            out_shape=pltpu.VMEM((tokens, inner), jnp.bfloat16),
            in_specs=[hbm] * len(args),
            out_specs=pl.BlockSpec(memory_space=pltpu.VMEM),
            scratch_shapes=[pltpu.VMEM(a.shape, a.dtype) for a in args] + [
                pltpu.VMEM((mp, tokens, x_proj.shape[1]), F32),
                pltpu.VMEM((states, tokens, LANES), F32),
                pltpu.VMEM((states, tokens, LANES), F32),
                pltpu.VMEM((blocks, states * SUB, LANES), F32),
                pltpu.VMEM((tokens, TILE), F32),
                pltpu.VMEM((blocks, tokens * SUB, LANES), F32),
                pltpu.VMEM((blocks, tokens * SUB, LANES), F32),
                pltpu.VMEM((blocks, tokens * SUB, LANES), F32),
                pltpu.VMEM((blocks, tokens * states * SUB, LANES), F32),
                pltpu.VMEM((blocks, states) + cell, F32),
                pltpu.VMEM((blocks,) + cell, F32),
                pltpu.VMEM((blocks, group) + cell, F32),
                pltpu.VMEM((blocks, group) + cell, F32),
                pltpu.VMEM((blocks, group) + cell, F32),
                pltpu.VMEM((blocks, group) + cell, F32),
                pltpu.VMEM((blocks, groups, 2) + cell, F32),
                pltpu.VMEM((blocks, 2) + cell, F32),
                dma((len(args),)),
                dma((mp - 1,)), dma((mp - 1,)),
                dma((blocks,)), dma((blocks,)),
                dma((blocks,)), dma((blocks,)),
                dma((blocks,)), dma((blocks,)),
                dma((blocks, groups)), dma((blocks, groups)),
            ],
            compiler_params=pltpu.CompilerParams(
                collective_id=0, has_side_effects=True,
                vmem_limit_bytes=58 * 1024 * 1024),
        )(*args)

    placed = (
        P("seq", "mp"),
        P("seq", "mp"),
        P("mp", None),
        P(None, "mp"),
        P("mp"),
        P(None, "mp"),
        P("mp"),
    )
    return jax.shard_map(
        per_device, mesh=mesh, in_specs=placed, out_specs=P("seq", "mp"), check_vma=False
    )
```

```python
import functools

import jax
import jax.numpy as jnp
from jax import lax
from jax.experimental import pallas as pl
from jax.experimental.pallas import tpu as pltpu
from jax.sharding import PartitionSpec as P

LANES = 128
SUB = 8
TILE = LANES * SUB
UNROLL = 8
HALF = 8
LOG2E = 1.4426950408889634
F32 = jnp.float32


def softplus(x):
    e = jnp.exp(-jnp.abs(x))
    series = e * (1.0 - e * (0.5 - e * (1.0 / 3.0 - e * (0.25 - e * 0.2))))
    return jnp.maximum(x, 0.0) + jnp.where(e < 0.03125, series, jnp.log(1.0 + e))


def kernel(seq, mp, tokens, inner, rank, states,
           u_hbm, g_hbm, xp_hbm, dtp_hbm, bias_hbm, alog_hbm, skip_hbm, out_ref,
           u_ref, g_ref, xp_ref, dtp_ref, bias_ref, alog_ref, skip_ref,
           proj, bs, cs, rate, raw, dts, drv, ys, fades, tot, sums, got_e, got_s, back, ent, far, near,
           in_sem, mp_send, mp_recv, e_send, e_recv, s_send, s_recv, b_send, b_recv,
           f_send, f_recv, here, ready):
    blocks = pl.cdiv(inner, TILE)
    parts = states // HALF
    subs = blocks * parts
    group = states
    groups = seq // group
    last = group - 1
    me = lax.axis_index("seq")
    my_mp = lax.axis_index("mp")
    mine = lax.rem(me, group)
    my_group = me // group
    base = my_group * group
    first = (group - SUB) // 2
    row = mine - first
    is_owner = jnp.logical_and(row >= 0, row < SUB)
    is_leader = my_mp == 0
    MESH = pl.DeviceIdType.MESH

    loads = [pltpu.make_async_copy(src, dst, in_sem.at[i]) for i, (src, dst) in enumerate((
        (u_hbm, u_ref), (xp_hbm, xp_ref), (alog_hbm, alog_ref), (dtp_hbm, dtp_ref),
        (bias_hbm, bias_ref), (g_hbm, g_ref), (skip_hbm, skip_ref)))]
    for load in loads:
        load.start()

    barrier = pltpu.get_barrier_semaphore()

    @pl.when(is_leader)
    def _():
        for m in range(1, mp):
            pl.semaphore_signal(barrier, inc=1, device_id={"mp": m}, device_id_type=MESH)

    @pl.when(my_mp > 0)
    def _():
        pl.semaphore_wait(barrier, 1)
        pl.semaphore_signal(here, inc=1, device_id={"mp": 0}, device_id_type=MESH)
        if mp > 2:
            pl.semaphore_wait(here, 1)

    @pl.when(is_leader)
    def _():
        pl.semaphore_wait(here, mp - 1)
        if mp > 2:
            for m in range(1, mp):
                pl.semaphore_signal(here, inc=1, device_id={"mp": m}, device_id_type=MESH)

        @pl.when(is_owner)
        def _():
            @pl.loop(1, group)
            def _(p):
                pl.semaphore_signal(barrier, inc=1,
                                    device_id={"seq": base + lax.rem(mine + p, group)},
                                    device_id_type=MESH)
            if groups > 1:
                @pl.loop(0, my_group)
                def _(g):
                    pl.semaphore_signal(barrier, inc=1, device_id={"seq": g * group + mine},
                                        device_id_type=MESH)

    def meet():
        @pl.when(is_leader)
        def _():
            @pl.when(is_owner)
            def _():
                pl.semaphore_wait(barrier, SUB - 1 + (groups - 1 - my_group))

            @pl.when(jnp.logical_not(is_owner))
            def _():
                pl.semaphore_wait(barrier, SUB)
            for m in range(1, mp):
                pl.semaphore_signal(ready, inc=1, device_id={"mp": m}, device_id_type=MESH)

        @pl.when(my_mp > 0)
        def _():
            pl.semaphore_wait(ready, 1)

    loads[0].wait()
    loads[1].wait()
    proj[my_mp] = lax.dot_general(u_ref[...], xp_ref[...], (((1,), (1,)), ((), ())),
                                  preferred_element_type=F32)
    shares = []
    for m in range(1, mp):
        copy = pltpu.make_async_remote_copy(
            src_ref=proj.at[my_mp], dst_ref=proj.at[my_mp],
            send_sem=mp_send.at[m - 1], recv_sem=mp_recv.at[m - 1],
            device_id={"mp": lax.rem(my_mp + m, mp)},
            device_id_type=MESH)
        copy.start()
        shares.append(copy)

    loads[2].wait()
    for k in range(blocks):
        for j in range(min(SUB, inner // LANES - k * SUB)):
            lo = (k * SUB + j) * LANES
            rate[k, pl.ds(j, states, stride=SUB), :] = (
                jnp.exp(alog_ref[:, lo:lo + LANES]) * (-LOG2E))
    loads[3].wait()
    loads[4].wait()

    for copy in shares:
        copy.wait()
    whole = proj[0]
    for m in range(1, mp):
        whole = whole + proj[m]
    low = whole[:, :rank].astype(jnp.bfloat16)

    def lanes_of(k):
        return min(SUB, inner // LANES - k * SUB)

    def tile(ref, k, i):
        return ref[k, pl.ds(pl.multiple_of(i * SUB, SUB), SUB), :]

    def rows_of(r):
        return pl.ds(pl.multiple_of(r * HALF, HALF), HALF)

    def steps(k):
        width = lanes_of(k) * LANES
        raw[:, :width] = jnp.dot(low, dtp_ref[:, k * TILE:k * TILE + width],
                                 preferred_element_type=F32)
        @pl.loop(0, lanes_of(k))
        def _(j):
            lo = pl.multiple_of((k * SUB + j) * LANES, LANES)
            cols = pl.ds(lo, LANES)
            dt = softplus(raw[:, pl.ds(pl.multiple_of(j * LANES, LANES), LANES)]
                          + bias_ref[:, cols])
            dts[k, pl.ds(j, tokens, stride=SUB), :] = dt
            drv[k, pl.ds(j, tokens, stride=SUB), :] = dt * u_ref[:, cols].astype(F32)
            sums[k, j] = jnp.sum(dt, axis=0, keepdims=True)

    def share_sums(k):
        @pl.when(is_owner)
        def _():
            got_s[k, mine] = sums[k, row]

        @pl.loop(0, SUB)
        def _(r):
            @pl.when(r != row)
            def _():
                pltpu.make_async_remote_copy(
                    src_ref=sums.at[k, r], dst_ref=got_s.at[k, mine],
                    send_sem=s_send.at[k], recv_sem=s_recv.at[k],
                    device_id={"seq": base + first + r}, device_id_type=MESH).start()

    def cell(t, n):
        return pl.ds(pl.multiple_of((t * states + n) * SUB, SUB), SUB)

    def ends(s):
        k, own_states = s // parts, range(s % parts * HALF, s % parts * HALF + HALF)
        rates = [rate[k, n * SUB:(n + 1) * SUB, :] for n in own_states]

        def body(it, hs):
            hs = list(hs)
            for i in range(UNROLL):
                t = it * UNROLL + i
                dt = tile(dts, k, t)
                dr = tile(drv, k, t)
                for i_n, n in enumerate(own_states):
                    fade = jnp.exp2(rates[i_n] * dt)
                    fades[k, cell(t, n), :] = fade
                    hs[i_n] = fade * hs[i_n] + bs[n, pl.ds(t, 1), :] * dr
            return tuple(hs)

        zero = jnp.zeros((SUB, LANES), F32)
        final = lax.fori_loop(0, tokens // UNROLL, body, (zero,) * HALF)
        for i_n in range(HALF):
            tot[s, pl.ds(i_n, SUB, stride=HALF), :] = final[i_n]

    def share_ends(s):
        @pl.when(is_owner)
        def _():
            got_e[s, mine] = tot[s, rows_of(row), :]

        @pl.when(jnp.logical_or(mine != last, groups > 1))
        def _():
            @pl.loop(0, SUB)
            def _(r):
                @pl.when(r != row)
                def _():
                    pltpu.make_async_remote_copy(
                        src_ref=tot.at[s, rows_of(r)], dst_ref=got_e.at[s, mine],
                        send_sem=e_send.at[s], recv_sem=e_recv.at[s, mine],
                        device_id={"seq": base + first + r}, device_id_type=MESH).start()

    def local(k):
        def body(it, hs):
            hs = list(hs)
            for i in range(UNROLL):
                t = it * UNROLL + i
                dr = tile(drv, k, t)
                acc = [None, None]
                for n in range(states):
                    hs[n] = fades[k, cell(t, n), :] * hs[n] + bs[n, pl.ds(t, 1), :] * dr
                    term = cs[n, pl.ds(t, 1), :] * hs[n]
                    acc[n % 2] = term if acc[n % 2] is None else acc[n % 2] + term
                ys[k, pl.ds(pl.multiple_of(t * SUB, SUB), SUB), :] = acc[0] + acc[1]
            return tuple(hs)

        zero = jnp.zeros((SUB, LANES), F32)
        lax.fori_loop(0, tokens // UNROLL, body, (zero,) * states)

    def drain(part, sem):
        pltpu.make_async_copy(part, part, sem).wait()

    def by_role(ref, owners, others, sem):
        @pl.when(is_owner)
        def _():
            drain(ref.at[pl.ds(0, owners)], sem)

        @pl.when(jnp.logical_not(is_owner))
        def _():
            drain(ref.at[pl.ds(0, others)], sem)

    def arrived(s, j):
        @pl.when(j != mine)
        def _():
            drain(got_e.at[s, j], e_recv.at[s, j])

    def own(s):
        k, h = s // parts, s % parts

        @pl.when(is_owner)
        def _():
            if h == 0:
                drain(got_s.at[k, pl.ds(0, group - 1)], s_recv.at[k])
            lo = jnp.minimum((k * SUB + row) * LANES, inner - LANES)
            rt = jnp.exp(alog_ref[h * HALF:(h + 1) * HALF, pl.ds(pl.multiple_of(lo, LANES), LANES)]
                         ) * (-LOG2E)
            carry = jnp.zeros((HALF, LANES), F32)
            if groups > 1:
                end, span = carry, carry
                for j in range(group):
                    arrived(s, j)
                    end = jnp.exp2(rt * got_s[k, j]) * end + got_e[s, j]
                    span = span + got_s[k, j]
                near[s, 0] = end
                near[s, 1] = span

                @pl.loop(my_group + 1, groups)
                def _(g):
                    pltpu.make_async_remote_copy(
                        src_ref=near.at[s], dst_ref=far.at[s, my_group],
                        send_sem=f_send.at[s, g], recv_sem=f_recv.at[s, my_group],
                        device_id={"seq": g * group + mine}, device_id_type=MESH).start()

                @pl.loop(my_group + 1, groups)
                def _(g):
                    drain(near.at[s], f_send.at[s, g])

                def follow(g, carry):
                    drain(far.at[s, g], f_recv.at[s, g])
                    return jnp.exp2(rt * far[s, g, 1]) * carry + far[s, g, 0]
                carry = lax.fori_loop(0, my_group, follow, carry)
            for j in range(group):
                if j > 0 or groups > 1:
                    @pl.when(j == mine)
                    def _(carry=carry):
                        ent[s, rows_of(row), :] = carry

                    @pl.when(j != mine)
                    def _(carry=carry, j=j):
                        back[s, j] = carry
                        pltpu.make_async_remote_copy(
                            src_ref=back.at[s, j], dst_ref=ent.at[s, rows_of(row)],
                            send_sem=b_send.at[s], recv_sem=b_recv.at[s],
                            device_id={"seq": base + j}, device_id_type=MESH).start()
                if j < last:
                    if groups == 1:
                        arrived(s, j)
                    carry = jnp.exp2(rt * got_s[k, j]) * carry + got_e[s, j]

    def correct(s):
        k, own_states = s // parts, range(s % parts * HALF, s % parts * HALF + HALF)

        @pl.when(jnp.logical_or(mine > 0, groups > 1))
        def _():
            by_role(ent.at[s], (SUB - 1) * HALF, SUB * HALF, b_recv.at[s])
            ents = [ent[s, pl.ds(i_n, SUB, stride=HALF), :] for i_n in range(HALF)]

            def body(it, es):
                es = list(es)
                for i in range(UNROLL):
                    t = it * UNROLL + i
                    acc = [tile(ys, k, t), None]
                    for i_n, n in enumerate(own_states):
                        es[i_n] = fades[k, cell(t, n), :] * es[i_n]
                        term = cs[n, pl.ds(t, 1), :] * es[i_n]
                        acc[i_n % 2] = term if acc[i_n % 2] is None else acc[i_n % 2] + term
                    ys[k, pl.ds(pl.multiple_of(t * SUB, SUB), SUB), :] = acc[0] + acc[1]
                return tuple(es)

            lax.fori_loop(0, tokens // UNROLL, body, tuple(ents))

    def finish(k):
        @pl.loop(0, lanes_of(k))
        def _(j):
            lo = pl.multiple_of((k * SUB + j) * LANES, LANES)
            cols = pl.ds(lo, LANES)
            y = ys[k, pl.ds(j, tokens, stride=SUB), :]
            g = g_ref[:, cols].astype(F32)
            mixed = (y + skip_ref[:, cols] * u_ref[:, cols].astype(F32)) * (
                g / (1.0 + jnp.exp(-g)))
            out_ref[:, cols] = mixed.astype(out_ref.dtype)

    if inner % TILE:
        sums[blocks - 1] = jnp.zeros((SUB, 1, LANES), F32)
    for n in range(states):
        bs[n] = jnp.broadcast_to(whole[:, rank + n:rank + n + 1], (tokens, LANES))
    for k in range(blocks):
        steps(k)
        for h in range(parts):
            ends(k * parts + h)
            if k == 0 and h == 0:
                meet()
            if h == 0:
                share_sums(k)
            share_ends(k * parts + h)
    for n in range(states):
        cs[n] = jnp.broadcast_to(
            whole[:, rank + states + n:rank + states + n + 1], (tokens, LANES))
    for k in range(blocks):
        local(k)
        for h in range(parts):
            own(k * parts + h)
    loads[5].wait()
    loads[6].wait()
    for k in range(blocks):
        for h in range(parts):
            correct(k * parts + h)
        finish(k)
    for k in range(blocks):
        by_role(sums.at[k], SUB - 1, SUB, s_send.at[k])
    for s in range(subs):
        @pl.when(jnp.logical_or(mine != last, groups > 1))
        def _(s=s):
            by_role(tot.at[s], (SUB - 1) * HALF, SUB * HALF, e_send.at[s])

        @pl.when(is_owner)
        def _(s=s):
            drain(back.at[s, pl.ds(0, group - 1 if groups > 1 else group - 2)], b_send.at[s])


def solution(mesh):
    seq, mp = mesh.shape["seq"], mesh.shape["mp"]

    def per_device(inner_act, gate_act, x_proj, dt_proj, dt_bias, a_log, skip):
        tokens, inner = inner_act.shape
        rank, states = dt_proj.shape[0], a_log.shape[0]
        blocks = pl.cdiv(inner, TILE)
        group, groups = states, seq // states
        subs = blocks * (states // HALF)
        hbm = pl.BlockSpec(memory_space=pltpu.MemorySpace.HBM)
        args = tuple(pltpu.with_memory_space_constraint(a, pltpu.HBM) for a in (
            inner_act, gate_act, x_proj.T, dt_proj, dt_bias.reshape(1, inner), a_log,
            skip.reshape(1, inner)))
        dma = pltpu.SemaphoreType.DMA
        return pl.pallas_call(
            functools.partial(kernel, seq, mp, tokens, inner, rank, states),
            out_shape=pltpu.VMEM((tokens, inner), jnp.bfloat16),
            in_specs=[hbm] * len(args),
            out_specs=pl.BlockSpec(memory_space=pltpu.VMEM),
            scratch_shapes=[pltpu.VMEM(a.shape, a.dtype) for a in args] + [
                pltpu.VMEM((mp, tokens, x_proj.shape[1]), F32),
                pltpu.VMEM((states, tokens, LANES), F32),
                pltpu.VMEM((states, tokens, LANES), F32),
                pltpu.VMEM((blocks, states * SUB, LANES), F32),
                pltpu.VMEM((tokens, TILE), F32),
                pltpu.VMEM((blocks, tokens * SUB, LANES), F32),
                pltpu.VMEM((blocks, tokens * SUB, LANES), F32),
                pltpu.VMEM((blocks, tokens * SUB, LANES), F32),
                pltpu.VMEM((blocks, tokens * states * SUB, LANES), F32),
                pltpu.VMEM((subs, SUB * HALF, LANES), F32),
                pltpu.VMEM((blocks, SUB, 1, LANES), F32),
                pltpu.VMEM((subs, group, HALF, LANES), F32),
                pltpu.VMEM((blocks, group, 1, LANES), F32),
                pltpu.VMEM((subs, group, HALF, LANES), F32),
                pltpu.VMEM((subs, SUB * HALF, LANES), F32),
                pltpu.VMEM((subs, groups, 2, HALF, LANES), F32),
                pltpu.VMEM((subs, 2, HALF, LANES), F32),
                dma((len(args),)),
                dma((mp - 1,)), dma((mp - 1,)),
                dma((subs,)), dma((subs, group)),
                dma((blocks,)), dma((blocks,)),
                dma((subs,)), dma((subs,)),
                dma((subs, groups)), dma((subs, groups)),
                pltpu.SemaphoreType.REGULAR, pltpu.SemaphoreType.REGULAR,
            ],
            compiler_params=pltpu.CompilerParams(
                collective_id=0, has_side_effects=True,
                vmem_limit_bytes=58 * 1024 * 1024),
        )(*args)

    placed = (
        P("seq", "mp"),
        P("seq", "mp"),
        P("mp", None),
        P(None, "mp"),
        P("mp"),
        P(None, "mp"),
        P("mp"),
    )
    return jax.shard_map(
        per_device, mesh=mesh, in_specs=placed, out_specs=P("seq", "mp"), check_vma=False
    )
```

```python
import functools

import jax
import jax.numpy as jnp
from jax import lax
from jax.experimental import pallas as pl
from jax.experimental.pallas import tpu as pltpu
from jax.sharding import PartitionSpec as P

LANES = 128
OWNERS = 8
SPOTS = (4, 11, 7, 8, 5, 10, 6, 9)
WAYS = 4
SPAN = 16
CUTS = 4
LOG2E = 1.4426950408889634
F32 = jnp.float32
BF16 = jnp.bfloat16
MESH = pl.DeviceIdType.MESH


def softplus(x):
    e = jnp.exp(-jnp.abs(x))
    series = e * (1.0 - e * (0.5 - e * (1.0 / 3.0 - e * (0.25 - e * 0.2))))
    return jnp.maximum(x, 0.0) + jnp.where(e < 0.03125, series, jnp.log(1.0 + e))


def at(start, size):
    return pl.ds(pl.multiple_of(start, size), size)


def kernel(seq, mp, tokens, inner, rank, states,
           u_hbm, g_hbm, xp_hbm, dtp_hbm, bias_hbm, alog_hbm, skip_hbm, out_ref,
           u_ref, g_ref, xp_ref, dtp_ref, bias_ref, alog_ref, skip_ref,
           proj, bl, cbd, rate, dts, drv, ys, fades, hist, tot, sums, got_e, got_s, back, ent,
           far, near, in_sem, cut_sem, mp_send, mp_recv, e_send, e_recv, s_send, s_recv, b_send,
           b_recv, f_send, f_recv, here, ready):
    blocks = inner // LANES
    rounds = pl.cdiv(blocks, OWNERS)
    group = len(SPOTS) * 2
    groups = seq // group
    last = group - 1
    half = states // 2
    me = lax.axis_index("seq")
    my_mp = lax.axis_index("mp")
    mine = lax.rem(me, group)
    my_group = me // group
    base = my_group * group
    row = sum(jnp.where(mine == spot, r, 0) for r, spot in enumerate(SPOTS))
    is_owner = jnp.logical_and(mine >= min(SPOTS), mine <= max(SPOTS))
    is_leader = my_mp == 0

    width = inner // CUTS
    firsts = []
    for c in range(CUTS):
        cols = pl.ds(c * width, width)
        for i, (src, dst) in enumerate(((u_hbm, u_ref), (xp_hbm, xp_ref))):
            firsts.append(pltpu.make_async_copy(src.at[:, cols], dst.at[:, cols],
                                                cut_sem.at[c, i]))
    loads = [pltpu.make_async_copy(src, dst, in_sem.at[i]) for i, (src, dst) in enumerate((
        (alog_hbm, alog_ref), (dtp_hbm, dtp_ref), (bias_hbm, bias_ref), (g_hbm, g_ref),
        (skip_hbm, skip_ref)))]
    for load in firsts + loads:
        load.start()

    barrier = pltpu.get_barrier_semaphore()

    @pl.when(is_leader)
    def _():
        for m in range(1, mp):
            pl.semaphore_signal(barrier, inc=1, device_id={"mp": m}, device_id_type=MESH)

    @pl.when(my_mp > 0)
    def _():
        pl.semaphore_wait(barrier, 1)
        pl.semaphore_signal(here, inc=1, device_id={"mp": 0}, device_id_type=MESH)
        if mp > 2:
            pl.semaphore_wait(here, 1)

    @pl.when(is_leader)
    def _():
        pl.semaphore_wait(here, mp - 1)
        if mp > 2:
            for m in range(1, mp):
                pl.semaphore_signal(here, inc=1, device_id={"mp": m}, device_id_type=MESH)

        @pl.when(is_owner)
        def _():
            @pl.loop(1, group)
            def _(p):
                pl.semaphore_signal(barrier, inc=1,
                                    device_id={"seq": base + lax.rem(mine + p, group)},
                                    device_id_type=MESH)
            if groups > 1:
                @pl.loop(0, my_group)
                def _(g):
                    pl.semaphore_signal(barrier, inc=1, device_id={"seq": g * group + mine},
                                        device_id_type=MESH)

    def meet():
        @pl.when(is_leader)
        def _():
            @pl.when(is_owner)
            def _():
                pl.semaphore_wait(barrier, OWNERS - 1 + (groups - 1 - my_group))

            @pl.when(jnp.logical_not(is_owner))
            def _():
                pl.semaphore_wait(barrier, OWNERS)
            for m in range(1, mp):
                pl.semaphore_signal(ready, inc=1, device_id={"mp": m}, device_id_type=MESH)

        @pl.when(my_mp > 0)
        def _():
            pl.semaphore_wait(ready, 1)

    part = None
    for c in range(CUTS):
        firsts[2 * c].wait()
        firsts[2 * c + 1].wait()
        cols = slice(c * width, (c + 1) * width)
        term = lax.dot_general(u_ref[:, cols], xp_ref[:, cols], (((1,), (1,)), ((), ())),
                               preferred_element_type=F32)
        part = term if part is None else part + term
    proj[my_mp] = part
    shares = []
    for m in range(1, mp):
        copy = pltpu.make_async_remote_copy(
            src_ref=proj.at[my_mp], dst_ref=proj.at[my_mp],
            send_sem=mp_send.at[m - 1], recv_sem=mp_recv.at[m - 1],
            device_id={"mp": lax.rem(my_mp + m, mp)},
            device_id_type=MESH)
        copy.start()
        shares.append(copy)

    for load in loads[:3]:
        load.wait()
    for b in range(blocks):
        rate[b] = jnp.exp(alog_ref[:, b * LANES:(b + 1) * LANES]) * (-LOG2E)

    for copy in shares:
        copy.wait()
    whole = proj[0]
    for m in range(1, mp):
        whole = whole + proj[m]
    low = whole[:, :rank].astype(BF16)

    def columns(b):
        return at(b * LANES, LANES)

    def steps():
        @pl.loop(0, blocks // WAYS)
        def _(q):
            raw = jnp.dot(low, dtp_ref[:, at(q * (WAYS * LANES), WAYS * LANES)],
                          preferred_element_type=F32)
            for i in range(WAYS):
                b = q * WAYS + i
                dt = softplus(raw[:, i * LANES:(i + 1) * LANES] + bias_ref[:, columns(b)])
                dts[b] = dt
                drv[b] = dt * u_ref[:, columns(b)].astype(F32)
                sums[lax.rem(b, OWNERS), b // OWNERS] = jnp.sum(dt, axis=0, keepdims=True)

    def spread():
        turned = whole[:, rank:rank + states].T
        for t in range(tokens):
            bl[t * states:(t + 1) * states, :] = jnp.broadcast_to(
                turned[:, t:t + 1], (states, LANES))

    def place():
        lane = lax.broadcasted_iota(jnp.int32, (whole.shape[1], SPAN * states), 1)
        line = lax.broadcasted_iota(jnp.int32, (whole.shape[1], SPAN * states), 0)
        pick = jnp.where(line == rank + states + lax.rem(lane, states), 1.0, 0.0).astype(BF16)
        wide = jnp.dot(whole.astype(BF16), pick, preferred_element_type=F32)
        lane = lax.broadcasted_iota(jnp.int32, wide.shape, 1)
        line = lax.broadcasted_iota(jnp.int32, wide.shape, 0)
        cbd[...] = jnp.where(lane // states == lax.rem(line, SPAN), wide, 0.0).astype(BF16)

    def share_sums():
        @pl.when(is_owner)
        def _():
            got_s[mine] = sums[row]
        for r, spot in enumerate(SPOTS):
            @pl.when(mine != spot)
            def _(r=r, spot=spot):
                pltpu.make_async_remote_copy(
                    src_ref=sums.at[r], dst_ref=got_s.at[mine], send_sem=s_send, recv_sem=s_recv,
                    device_id={"seq": base + spot}, device_id_type=MESH).start()

    def ends(q):
        ours = range(q * WAYS, (q + 1) * WAYS)
        rates = [[rate[b, v * half:(v + 1) * half, :] for v in range(2)] for b in ours]

        def body(it, hs):
            hs = list(hs)
            for i in range(SPAN):
                t = it * SPAN + i
                bb = [bl[at(t * states + v * half, half), :] for v in range(2)]
                for w, b in enumerate(ours):
                    dt = dts[b, pl.ds(t, 1), :]
                    dr = drv[b, pl.ds(t, 1), :]
                    for v in range(2):
                        fade = jnp.exp2(rates[w][v] * dt)
                        fades[b, at(t * states + v * half, half), :] = fade
                        hs[2 * w + v] = fade * hs[2 * w + v] + bb[v] * dr
            return tuple(hs)

        zero = jnp.zeros((half, LANES), F32)
        final = lax.fori_loop(0, tokens // SPAN, body, (zero,) * (2 * WAYS))
        for w, b in enumerate(ours):
            for v in range(2):
                tot[b, v * half:(v + 1) * half, :] = final[2 * w + v]

    def sends_end():
        return jnp.logical_or(mine != last, groups > 1)

    def share_ends(q):
        for b in range(q * WAYS, (q + 1) * WAYS):
            spot = SPOTS[b % OWNERS]

            @pl.when(mine == spot)
            def _(b=b):
                got_e[b // OWNERS, mine] = tot[b]

            @pl.when(jnp.logical_and(mine != spot, sends_end()))
            def _(b=b, spot=spot):
                pltpu.make_async_remote_copy(
                    src_ref=tot.at[b], dst_ref=got_e.at[b // OWNERS, mine],
                    send_sem=e_send.at[b], recv_sem=e_recv.at[b // OWNERS, mine],
                    device_id={"seq": base + spot}, device_id_type=MESH).start()

    def weigh(ours, add):
        @pl.loop(0, tokens // SPAN)
        def _(g):
            c = cbd[at(g * SPAN, SPAN), :]
            h = jnp.concatenate([hist[w, at(g * (SPAN * states), SPAN * states), :]
                                 for w in range(len(ours))], axis=1)
            y = jnp.dot(c, h, preferred_element_type=F32)
            for w, b in enumerate(ours):
                term = y[:, w * LANES:(w + 1) * LANES]
                here_t = at(g * SPAN, SPAN)
                ys[b, here_t, :] = ys[b, here_t, :] + term if add else term

    def local(ours):
        def body(it, hs):
            hs = list(hs)
            for i in range(SPAN // 2):
                t = it * (SPAN // 2) + i
                bb = [bl[at(t * states + v * half, half), :] for v in range(2)]
                for w, b in enumerate(ours):
                    dr = drv[b, pl.ds(t, 1), :]
                    for v in range(2):
                        fade = fades[b, at(t * states + v * half, half), :]
                        hs[2 * w + v] = fade * hs[2 * w + v] + bb[v] * dr
                    hist[w, at(t * states, states), :] = jnp.concatenate(
                        hs[2 * w:2 * w + 2], axis=0).astype(BF16)
            return tuple(hs)

        zero = jnp.zeros((half, LANES), F32)
        lax.fori_loop(0, tokens // (SPAN // 2), body, (zero,) * (2 * len(ours)))
        weigh(ours, False)

    def drain(part, sem):
        pltpu.make_async_copy(part, part, sem).wait()

    def arrived(k, j):
        @pl.when(j != mine)
        def _():
            drain(got_e.at[k, j], e_recv.at[k, j])

    def own(k):
        has = jnp.logical_and(is_owner, k * OWNERS + row < blocks)

        if k == 0:
            @pl.when(is_owner)
            def _():
                drain(got_s.at[pl.ds(0, group - 1)], s_recv)

        @pl.when(has)
        def _():
            rt = rate[k * OWNERS + row]
            carry = jnp.zeros((states, LANES), F32)
            if groups > 1:
                end, span = carry, carry
                for j in range(group):
                    arrived(k, j)
                    end = jnp.exp2(rt * got_s[j, k]) * end + got_e[k, j]
                    span = span + got_s[j, k]
                near[k, 0] = end
                near[k, 1] = span

                @pl.loop(my_group + 1, groups)
                def _(g):
                    pltpu.make_async_remote_copy(
                        src_ref=near.at[k], dst_ref=far.at[k, my_group],
                        send_sem=f_send.at[k, g], recv_sem=f_recv.at[k, my_group],
                        device_id={"seq": g * group + mine}, device_id_type=MESH).start()

                @pl.loop(my_group + 1, groups)
                def _(g):
                    drain(near.at[k], f_send.at[k, g])

                def follow(g, carry):
                    drain(far.at[k, g], f_recv.at[k, g])
                    return jnp.exp2(rt * far[k, g, 1]) * carry + far[k, g, 0]
                carry = lax.fori_loop(0, my_group, follow, carry)
            for j in range(group):
                if j > 0 or groups > 1:
                    @pl.when(j == mine)
                    def _(carry=carry):
                        ent[k * OWNERS + row] = carry

                    @pl.when(j != mine)
                    def _(carry=carry, j=j):
                        back[k, j] = carry
                        pltpu.make_async_remote_copy(
                            src_ref=back.at[k, j], dst_ref=ent.at[k * OWNERS + row],
                            send_sem=b_send.at[k], recv_sem=b_recv.at[k * OWNERS + row],
                            device_id={"seq": base + j}, device_id_type=MESH).start()
                if j < last:
                    if groups == 1:
                        arrived(k, j)
                    carry = jnp.exp2(rt * got_s[j, k]) * carry + got_e[k, j]

    def correct(ours):
        @pl.when(jnp.logical_or(mine > 0, groups > 1))
        def _():
            for b in ours:
                @pl.when(mine != SPOTS[b % OWNERS])
                def _(b=b):
                    drain(ent.at[b], b_recv.at[b])
            enters = tuple(ent[b, v * half:(v + 1) * half, :] for b in ours for v in range(2))

            def body(it, es):
                es = list(es)
                for i in range(SPAN // 2):
                    t = it * (SPAN // 2) + i
                    for w, b in enumerate(ours):
                        for v in range(2):
                            fade = fades[b, at(t * states + v * half, half), :]
                            es[2 * w + v] = fade * es[2 * w + v]
                        hist[w, at(t * states, states), :] = jnp.concatenate(
                            es[2 * w:2 * w + 2], axis=0).astype(BF16)
                return tuple(es)

            lax.fori_loop(0, tokens // (SPAN // 2), body, enters)
            weigh(ours, True)

    def finish(ours):
        @pl.loop(ours[0], ours[-1] + 1)
        def _(b):
            cols = columns(b)
            g = g_ref[:, cols].astype(F32)
            mixed = (ys[b] + skip_ref[:, cols] * u_ref[:, cols].astype(F32)) * (
                g / (1.0 + jnp.exp(-g)))
            out_ref[:, cols] = mixed.astype(out_ref.dtype)

    chunks = [range(lo, min(lo + OWNERS, blocks)) for lo in range(0, blocks, OWNERS)]
    pieces = chunks[:-1] + [range(lo, lo + WAYS) for lo in range(chunks[-1][0], blocks, WAYS)]
    if blocks % OWNERS:
        for r in range(blocks % OWNERS, OWNERS):
            sums[r, rounds - 1] = jnp.zeros((1, LANES), F32)
    steps()
    spread()
    for q in range(blocks // WAYS):
        ends(q)
        if q == 0:
            meet()
            share_sums()
        share_ends(q)
    place()
    for k, ours in enumerate(chunks):
        local(ours)
        own(k)
    loads[3].wait()
    loads[4].wait()
    for ours in pieces:
        correct(ours)
        finish(ours)

    @pl.when(is_owner)
    def _():
        drain(sums.at[pl.ds(0, OWNERS - 1)], s_send)

    @pl.when(jnp.logical_not(is_owner))
    def _():
        drain(sums, s_send)
    for b in range(blocks):
        @pl.when(jnp.logical_and(mine != SPOTS[b % OWNERS], sends_end()))
        def _(b=b):
            drain(tot.at[b], e_send.at[b])
    for k in range(rounds):
        @pl.when(jnp.logical_and(is_owner, k * OWNERS + row < blocks))
        def _(k=k):
            drain(back.at[k, pl.ds(0, group - 1 if groups > 1 else group - 2)], b_send.at[k])


def solution(mesh):
    seq, mp = mesh.shape["seq"], mesh.shape["mp"]

    def per_device(inner_act, gate_act, x_proj, dt_proj, dt_bias, a_log, skip):
        tokens, inner = inner_act.shape
        rank, states = dt_proj.shape[0], a_log.shape[0]
        blocks = inner // LANES
        rounds = pl.cdiv(blocks, OWNERS)
        group = len(SPOTS) * 2
        groups = seq // group
        hbm = pl.BlockSpec(memory_space=pltpu.MemorySpace.HBM)
        args = tuple(pltpu.with_memory_space_constraint(a, pltpu.HBM) for a in (
            inner_act, gate_act, x_proj.T, dt_proj, dt_bias.reshape(1, inner), a_log,
            skip.reshape(1, inner)))
        cell = (states, LANES)
        dma = pltpu.SemaphoreType.DMA
        return pl.pallas_call(
            functools.partial(kernel, seq, mp, tokens, inner, rank, states),
            out_shape=pltpu.VMEM((tokens, inner), jnp.bfloat16),
            in_specs=[hbm] * len(args),
            out_specs=pl.BlockSpec(memory_space=pltpu.VMEM),
            scratch_shapes=[pltpu.VMEM(a.shape, a.dtype) for a in args] + [
                pltpu.VMEM((mp, tokens, x_proj.shape[1]), F32),
                pltpu.VMEM((tokens * states, LANES), F32),
                pltpu.VMEM((tokens, SPAN * states), BF16),
                pltpu.VMEM((blocks,) + cell, F32),
                pltpu.VMEM((blocks, tokens, LANES), F32),
                pltpu.VMEM((blocks, tokens, LANES), F32),
                pltpu.VMEM((blocks, tokens, LANES), F32),
                pltpu.VMEM((blocks, tokens * states, LANES), F32),
                pltpu.VMEM((OWNERS, tokens * states, LANES), BF16),
                pltpu.VMEM((blocks,) + cell, F32),
                pltpu.VMEM((OWNERS, rounds, 1, LANES), F32),
                pltpu.VMEM((rounds, group) + cell, F32),
                pltpu.VMEM((group, rounds, 1, LANES), F32),
                pltpu.VMEM((rounds, group) + cell, F32),
                pltpu.VMEM((blocks,) + cell, F32),
                pltpu.VMEM((rounds, groups, 2) + cell, F32),
                pltpu.VMEM((rounds, 2) + cell, F32),
                dma((5,)), dma((CUTS, 2)),
                dma((mp - 1,)), dma((mp - 1,)),
                dma((blocks,)), dma((rounds, group)),
                dma, dma,
                dma((rounds,)), dma((blocks,)),
                dma((rounds, groups)), dma((rounds, groups)),
                pltpu.SemaphoreType.REGULAR, pltpu.SemaphoreType.REGULAR,
            ],
            compiler_params=pltpu.CompilerParams(
                collective_id=0, has_side_effects=True,
                vmem_limit_bytes=58 * 1024 * 1024),
        )(*args)

    placed = (
        P("seq", "mp"),
        P("seq", "mp"),
        P("mp", None),
        P(None, "mp"),
        P("mp"),
        P(None, "mp"),
        P("mp"),
    )
    return jax.shard_map(
        per_device, mesh=mesh, in_specs=placed, out_specs=P("seq", "mp"), check_vma=False
    )
```

```python
import functools

import jax
import jax.numpy as jnp
from jax import lax
from jax.experimental import pallas as pl
from jax.experimental.pallas import tpu as pltpu
from jax.sharding import PartitionSpec as P

LANES = 128
OWNERS = 8
SPOTS = (4, 11, 7, 8, 5, 10, 6, 9)
WAYS = 4
SPAN = 16
CUTS = 4
LOG2E = 1.4426950408889634
F32 = jnp.float32
BF16 = jnp.bfloat16
MESH = pl.DeviceIdType.MESH


def softplus(x):
    e = jnp.exp(-jnp.abs(x))
    series = e * (1.0 - e * (0.5 - e * (1.0 / 3.0 - e * (0.25 - e * 0.2))))
    return jnp.maximum(x, 0.0) + jnp.where(e < 0.03125, series, jnp.log(1.0 + e))


def at(start, size):
    return pl.ds(pl.multiple_of(start, size), size)


def kernel(seq, mp, tokens, inner, rank, states,
           u_hbm, g_hbm, xp_hbm, dtp_hbm, bias_hbm, alog_hbm, skip_hbm, out_ref,
           u_ref, g_ref, xp_ref, dtp_ref, bias_ref, alog_ref, skip_ref,
           proj, bl, cbd, rate, dts, drv, ys, fades, hist, tot, sums, got_e, got_s, back, ent,
           far, near, in_sem, cut_sem, mp_send, mp_recv, e_send, e_recv, s_send, s_recv, b_send,
           b_recv, f_send, f_recv, here, ready):
    blocks = inner // LANES
    rounds = pl.cdiv(blocks, OWNERS)
    group = len(SPOTS) * 2
    groups = seq // group
    last = group - 1
    half = states // 2
    me = lax.axis_index("seq")
    my_mp = lax.axis_index("mp")
    mine = lax.rem(me, group)
    my_group = me // group
    base = my_group * group
    row = sum(jnp.where(mine == spot, r, 0) for r, spot in enumerate(SPOTS))
    is_owner = jnp.logical_and(mine >= min(SPOTS), mine <= max(SPOTS))
    is_leader = my_mp == 0

    width = inner // CUTS
    firsts = []
    for c in range(CUTS):
        cols = pl.ds(c * width, width)
        for i, (src, dst) in enumerate(((u_hbm, u_ref), (xp_hbm, xp_ref))):
            firsts.append(pltpu.make_async_copy(src.at[:, cols], dst.at[:, cols],
                                                cut_sem.at[c, i]))
    loads = [pltpu.make_async_copy(src, dst, in_sem.at[i]) for i, (src, dst) in enumerate((
        (alog_hbm, alog_ref), (dtp_hbm, dtp_ref), (bias_hbm, bias_ref), (g_hbm, g_ref),
        (skip_hbm, skip_ref)))]
    for load in firsts + loads:
        load.start()

    barrier = pltpu.get_barrier_semaphore()

    @pl.when(is_leader)
    def _():
        for m in range(1, mp):
            pl.semaphore_signal(barrier, inc=1, device_id={"mp": m}, device_id_type=MESH)

    @pl.when(my_mp > 0)
    def _():
        pl.semaphore_wait(barrier, 1)
        pl.semaphore_signal(here, inc=1, device_id={"mp": 0}, device_id_type=MESH)
        if mp > 2:
            pl.semaphore_wait(here, 1)

    @pl.when(is_leader)
    def _():
        pl.semaphore_wait(here, mp - 1)
        if mp > 2:
            for m in range(1, mp):
                pl.semaphore_signal(here, inc=1, device_id={"mp": m}, device_id_type=MESH)

        @pl.when(is_owner)
        def _():
            @pl.loop(1, group)
            def _(p):
                pl.semaphore_signal(barrier, inc=1,
                                    device_id={"seq": base + lax.rem(mine + p, group)},
                                    device_id_type=MESH)
            if groups > 1:
                @pl.loop(0, my_group)
                def _(g):
                    pl.semaphore_signal(barrier, inc=1, device_id={"seq": g * group + mine},
                                        device_id_type=MESH)

    def meet():
        @pl.when(is_leader)
        def _():
            @pl.when(is_owner)
            def _():
                pl.semaphore_wait(barrier, OWNERS - 1 + (groups - 1 - my_group))

            @pl.when(jnp.logical_not(is_owner))
            def _():
                pl.semaphore_wait(barrier, OWNERS)
            for m in range(1, mp):
                pl.semaphore_signal(ready, inc=1, device_id={"mp": m}, device_id_type=MESH)

        @pl.when(my_mp > 0)
        def _():
            pl.semaphore_wait(ready, 1)

    part = None
    for c in range(CUTS):
        firsts[2 * c].wait()
        firsts[2 * c + 1].wait()
        cols = slice(c * width, (c + 1) * width)
        term = lax.dot_general(u_ref[:, cols], xp_ref[:, cols], (((1,), (1,)), ((), ())),
                               preferred_element_type=F32)
        part = term if part is None else part + term
    proj[my_mp] = part
    shares = []
    for m in range(1, mp):
        copy = pltpu.make_async_remote_copy(
            src_ref=proj.at[my_mp], dst_ref=proj.at[my_mp],
            send_sem=mp_send.at[m - 1], recv_sem=mp_recv.at[m - 1],
            device_id={"mp": lax.rem(my_mp + m, mp)},
            device_id_type=MESH)
        copy.start()
        shares.append(copy)

    for load in loads[:3]:
        load.wait()
    for b in range(blocks):
        rate[b] = jnp.exp(alog_ref[:, b * LANES:(b + 1) * LANES]) * (-LOG2E)

    for copy in shares:
        copy.wait()
    whole = proj[0]
    for m in range(1, mp):
        whole = whole + proj[m]
    low = whole[:, :rank].astype(BF16)

    def columns(b):
        return at(b * LANES, LANES)

    def steps():
        @pl.loop(0, blocks // WAYS)
        def _(q):
            raw = jnp.dot(low, dtp_ref[:, at(q * (WAYS * LANES), WAYS * LANES)],
                          preferred_element_type=F32)
            for i in range(WAYS):
                b = q * WAYS + i
                dt = softplus(raw[:, i * LANES:(i + 1) * LANES] + bias_ref[:, columns(b)])
                dts[b] = dt
                drv[b] = dt * u_ref[:, columns(b)].astype(F32)
                sums[lax.rem(b, OWNERS), b // OWNERS] = jnp.sum(dt, axis=0, keepdims=True)

    def spread():
        turned = whole[:, rank:rank + states].T
        for t in range(tokens):
            bl[t * states:(t + 1) * states, :] = jnp.broadcast_to(
                turned[:, t:t + 1], (states, LANES))

    def place():
        lane = lax.broadcasted_iota(jnp.int32, (whole.shape[1], SPAN * states), 1)
        line = lax.broadcasted_iota(jnp.int32, (whole.shape[1], SPAN * states), 0)
        pick = jnp.where(line == rank + states + lax.rem(lane, states), 1.0, 0.0).astype(BF16)
        wide = jnp.dot(whole.astype(BF16), pick, preferred_element_type=F32)
        lane = lax.broadcasted_iota(jnp.int32, wide.shape, 1)
        line = lax.broadcasted_iota(jnp.int32, wide.shape, 0)
        cbd[...] = jnp.where(lane // states == lax.rem(line, SPAN), wide, 0.0).astype(BF16)

    def share_sums():
        @pl.when(is_owner)
        def _():
            got_s[mine] = sums[row]
        for r, spot in enumerate(SPOTS):
            @pl.when(mine != spot)
            def _(r=r, spot=spot):
                pltpu.make_async_remote_copy(
                    src_ref=sums.at[r], dst_ref=got_s.at[mine], send_sem=s_send, recv_sem=s_recv,
                    device_id={"seq": base + spot}, device_id_type=MESH).start()

    def ends(q):
        ours = range(q * WAYS, (q + 1) * WAYS)
        rates = [[rate[b, v * half:(v + 1) * half, :] for v in range(2)] for b in ours]

        def body(it, hs):
            hs = list(hs)
            for i in range(SPAN):
                t = it * SPAN + i
                bb = [bl[at(t * states + v * half, half), :] for v in range(2)]
                for w, b in enumerate(ours):
                    dt = dts[b, pl.ds(t, 1), :]
                    dr = drv[b, pl.ds(t, 1), :]
                    for v in range(2):
                        fade = jnp.exp2(rates[w][v] * dt)
                        fades[b, at(t * states + v * half, half), :] = fade
                        hs[2 * w + v] = fade * hs[2 * w + v] + bb[v] * dr
            return tuple(hs)

        zero = jnp.zeros((half, LANES), F32)
        final = lax.fori_loop(0, tokens // SPAN, body, (zero,) * (2 * WAYS))
        for w, b in enumerate(ours):
            for v in range(2):
                tot[b, v * half:(v + 1) * half, :] = final[2 * w + v]

    def sends_end():
        return jnp.logical_or(mine != last, groups > 1)

    def share_ends(q):
        for b in range(q * WAYS, (q + 1) * WAYS):
            spot = SPOTS[b % OWNERS]

            @pl.when(mine == spot)
            def _(b=b):
                got_e[b // OWNERS, mine] = tot[b]

            @pl.when(jnp.logical_and(mine != spot, sends_end()))
            def _(b=b, spot=spot):
                pltpu.make_async_remote_copy(
                    src_ref=tot.at[b], dst_ref=got_e.at[b // OWNERS, mine],
                    send_sem=e_send.at[b], recv_sem=e_recv.at[b // OWNERS, mine],
                    device_id={"seq": base + spot}, device_id_type=MESH).start()

    def weigh(ours, add):
        for g in range(tokens // SPAN):
            here_t = slice(g * SPAN, (g + 1) * SPAN)
            past = slice(g * SPAN * states, (g + 1) * SPAN * states)
            h = jnp.concatenate([hist[w, past, :] for w in range(len(ours))], axis=1)
            y = jnp.dot(cbd[here_t, :], h, preferred_element_type=F32)
            for w, b in enumerate(ours):
                term = y[:, w * LANES:(w + 1) * LANES]
                ys[b, here_t, :] = ys[b, here_t, :] + term if add else term

    def local(ours):
        def body(it, hs):
            hs = list(hs)
            for i in range(SPAN // 2):
                t = it * (SPAN // 2) + i
                bb = [bl[at(t * states + v * half, half), :] for v in range(2)]
                for w, b in enumerate(ours):
                    dr = drv[b, pl.ds(t, 1), :]
                    for v in range(2):
                        fade = fades[b, at(t * states + v * half, half), :]
                        hs[2 * w + v] = fade * hs[2 * w + v] + bb[v] * dr
                    hist[w, at(t * states, states), :] = jnp.concatenate(
                        hs[2 * w:2 * w + 2], axis=0).astype(BF16)
            return tuple(hs)

        zero = jnp.zeros((half, LANES), F32)
        lax.fori_loop(0, tokens // (SPAN // 2), body, (zero,) * (2 * len(ours)))
        weigh(ours, False)

    def drain(part, sem):
        pltpu.make_async_copy(part, part, sem).wait()

    def arrived(k, j):
        @pl.when(j != mine)
        def _():
            drain(got_e.at[k, j], e_recv.at[k, j])

    def own(k):
        has = jnp.logical_and(is_owner, k * OWNERS + row < blocks)

        if k == 0:
            @pl.when(is_owner)
            def _():
                drain(got_s.at[pl.ds(0, group - 1)], s_recv)

        @pl.when(has)
        def _():
            rt = rate[k * OWNERS + row]
            carry = jnp.zeros((states, LANES), F32)
            if groups > 1:
                end, span = carry, carry
                for j in range(group):
                    arrived(k, j)
                    end = jnp.exp2(rt * got_s[j, k]) * end + got_e[k, j]
                    span = span + got_s[j, k]
                near[k, 0] = end
                near[k, 1] = span

                @pl.loop(my_group + 1, groups)
                def _(g):
                    pltpu.make_async_remote_copy(
                        src_ref=near.at[k], dst_ref=far.at[k, my_group],
                        send_sem=f_send.at[k, g], recv_sem=f_recv.at[k, my_group],
                        device_id={"seq": g * group + mine}, device_id_type=MESH).start()

                @pl.loop(my_group + 1, groups)
                def _(g):
                    drain(near.at[k], f_send.at[k, g])

                def follow(g, carry):
                    drain(far.at[k, g], f_recv.at[k, g])
                    return jnp.exp2(rt * far[k, g, 1]) * carry + far[k, g, 0]
                carry = lax.fori_loop(0, my_group, follow, carry)
            for j in range(group):
                if j > 0 or groups > 1:
                    @pl.when(j == mine)
                    def _(carry=carry):
                        ent[k * OWNERS + row] = carry

                    @pl.when(j != mine)
                    def _(carry=carry, j=j):
                        back[k, j] = carry
                        pltpu.make_async_remote_copy(
                            src_ref=back.at[k, j], dst_ref=ent.at[k * OWNERS + row],
                            send_sem=b_send.at[k], recv_sem=b_recv.at[k * OWNERS + row],
                            device_id={"seq": base + j}, device_id_type=MESH).start()
                if j < last:
                    if groups == 1:
                        arrived(k, j)
                    carry = jnp.exp2(rt * got_s[j, k]) * carry + got_e[k, j]

    def correct(ours):
        @pl.when(jnp.logical_or(mine > 0, groups > 1))
        def _():
            for b in ours:
                @pl.when(mine != SPOTS[b % OWNERS])
                def _(b=b):
                    drain(ent.at[b], b_recv.at[b])
            enters = tuple(ent[b, v * half:(v + 1) * half, :] for b in ours for v in range(2))

            def body(it, es):
                es = list(es)
                for i in range(SPAN // 2):
                    t = it * (SPAN // 2) + i
                    for w, b in enumerate(ours):
                        for v in range(2):
                            fade = fades[b, at(t * states + v * half, half), :]
                            es[2 * w + v] = fade * es[2 * w + v]
                        hist[w, at(t * states, states), :] = jnp.concatenate(
                            es[2 * w:2 * w + 2], axis=0).astype(BF16)
                return tuple(es)

            lax.fori_loop(0, tokens // (SPAN // 2), body, enters)
            weigh(ours, True)

    def finish(ours):
        @pl.loop(ours[0], ours[-1] + 1)
        def _(b):
            cols = columns(b)
            g = g_ref[:, cols].astype(F32)
            mixed = (ys[b] + skip_ref[:, cols] * u_ref[:, cols].astype(F32)) * (
                g / (1.0 + jnp.exp(-g)))
            out_ref[:, cols] = mixed.astype(out_ref.dtype)

    chunks = [range(lo, min(lo + OWNERS, blocks)) for lo in range(0, blocks, OWNERS)]
    pieces = chunks[:-1] + [range(lo, lo + WAYS) for lo in range(chunks[-1][0], blocks, WAYS)]
    if blocks % OWNERS:
        for r in range(blocks % OWNERS, OWNERS):
            sums[r, rounds - 1] = jnp.zeros((1, LANES), F32)
    steps()
    spread()
    for q in range(blocks // WAYS):
        ends(q)
        if q == 0:
            meet()
            share_sums()
        share_ends(q)
    place()
    for k, ours in enumerate(chunks):
        local(ours)
        own(k)
    loads[3].wait()
    loads[4].wait()
    for ours in pieces:
        correct(ours)
        finish(ours)

    @pl.when(is_owner)
    def _():
        drain(sums.at[pl.ds(0, OWNERS - 1)], s_send)

    @pl.when(jnp.logical_not(is_owner))
    def _():
        drain(sums, s_send)
    for b in range(blocks):
        @pl.when(jnp.logical_and(mine != SPOTS[b % OWNERS], sends_end()))
        def _(b=b):
            drain(tot.at[b], e_send.at[b])
    for k in range(rounds):
        @pl.when(jnp.logical_and(is_owner, k * OWNERS + row < blocks))
        def _(k=k):
            drain(back.at[k, pl.ds(0, group - 1 if groups > 1 else group - 2)], b_send.at[k])


def solution(mesh):
    seq, mp = mesh.shape["seq"], mesh.shape["mp"]

    def per_device(inner_act, gate_act, x_proj, dt_proj, dt_bias, a_log, skip):
        tokens, inner = inner_act.shape
        rank, states = dt_proj.shape[0], a_log.shape[0]
        blocks = inner // LANES
        rounds = pl.cdiv(blocks, OWNERS)
        group = len(SPOTS) * 2
        groups = seq // group
        hbm = pl.BlockSpec(memory_space=pltpu.MemorySpace.HBM)
        args = tuple(pltpu.with_memory_space_constraint(a, pltpu.HBM) for a in (
            inner_act, gate_act, x_proj.T, dt_proj, dt_bias.reshape(1, inner), a_log,
            skip.reshape(1, inner)))
        cell = (states, LANES)
        dma = pltpu.SemaphoreType.DMA
        return pl.pallas_call(
            functools.partial(kernel, seq, mp, tokens, inner, rank, states),
            out_shape=pltpu.VMEM((tokens, inner), jnp.bfloat16),
            in_specs=[hbm] * len(args),
            out_specs=pl.BlockSpec(memory_space=pltpu.VMEM),
            scratch_shapes=[pltpu.VMEM(a.shape, a.dtype) for a in args] + [
                pltpu.VMEM((mp, tokens, x_proj.shape[1]), F32),
                pltpu.VMEM((tokens * states, LANES), F32),
                pltpu.VMEM((tokens, SPAN * states), BF16),
                pltpu.VMEM((blocks,) + cell, F32),
                pltpu.VMEM((blocks, tokens, LANES), F32),
                pltpu.VMEM((blocks, tokens, LANES), F32),
                pltpu.VMEM((blocks, tokens, LANES), F32),
                pltpu.VMEM((blocks, tokens * states, LANES), F32),
                pltpu.VMEM((OWNERS, tokens * states, LANES), BF16),
                pltpu.VMEM((blocks,) + cell, F32),
                pltpu.VMEM((OWNERS, rounds, 1, LANES), F32),
                pltpu.VMEM((rounds, group) + cell, F32),
                pltpu.VMEM((group, rounds, 1, LANES), F32),
                pltpu.VMEM((rounds, group) + cell, F32),
                pltpu.VMEM((blocks,) + cell, F32),
                pltpu.VMEM((rounds, groups, 2) + cell, F32),
                pltpu.VMEM((rounds, 2) + cell, F32),
                dma((5,)), dma((CUTS, 2)),
                dma((mp - 1,)), dma((mp - 1,)),
                dma((blocks,)), dma((rounds, group)),
                dma, dma,
                dma((rounds,)), dma((blocks,)),
                dma((rounds, groups)), dma((rounds, groups)),
                pltpu.SemaphoreType.REGULAR, pltpu.SemaphoreType.REGULAR,
            ],
            compiler_params=pltpu.CompilerParams(
                collective_id=0, has_side_effects=True,
                vmem_limit_bytes=58 * 1024 * 1024),
        )(*args)

    placed = (
        P("seq", "mp"),
        P("seq", "mp"),
        P("mp", None),
        P(None, "mp"),
        P("mp"),
        P(None, "mp"),
        P("mp"),
    )
    return jax.shard_map(
        per_device, mesh=mesh, in_specs=placed, out_specs=P("seq", "mp"), check_vma=False
    )
```

```python
import functools

import jax
import jax.numpy as jnp
from jax import lax
from jax.experimental import pallas as pl
from jax.experimental.pallas import tpu as pltpu
from jax.sharding import PartitionSpec as P

LANES = 128
OWNERS = 8
SPOTS = (4, 11, 7, 8, 5, 10, 6, 9)
WAYS = 4
SPAN = 16
CUTS = 4
LOG2E = 1.4426950408889634
F32 = jnp.float32
BF16 = jnp.bfloat16
MESH = pl.DeviceIdType.MESH


def softplus(x):
    e = jnp.exp(-jnp.abs(x))
    series = e * (1.0 - e * (0.5 - e * (1.0 / 3.0 - e * (0.25 - e * 0.2))))
    return jnp.maximum(x, 0.0) + jnp.where(e < 0.03125, series, jnp.log(1.0 + e))


def at(start, size):
    return pl.ds(pl.multiple_of(start, size), size)


def kernel(seq, mp, tokens, inner, rank, states,
           u_hbm, g_hbm, xp_hbm, dtp_hbm, bias_hbm, alog_hbm, skip_hbm, out_ref,
           u_ref, g_ref, xp_ref, dtp_ref, bias_ref, alog_ref, skip_ref,
           proj, bl, cbd, rate, dts, drv, ys, hist, gone, tot, sums, got_e, got_s, back, ent,
           far, near, in_sem, cut_sem, mp_send, mp_recv, e_send, e_recv, s_send, s_recv, b_send,
           b_recv, f_send, f_recv, here, ready):
    blocks = inner // LANES
    rounds = pl.cdiv(blocks, OWNERS)
    group = len(SPOTS) * 2
    groups = seq // group
    last = group - 1
    half = states // 2
    me = lax.axis_index("seq")
    my_mp = lax.axis_index("mp")
    mine = lax.rem(me, group)
    my_group = me // group
    base = my_group * group
    row = sum(jnp.where(mine == spot, r, 0) for r, spot in enumerate(SPOTS))
    is_owner = jnp.logical_and(mine >= min(SPOTS), mine <= max(SPOTS))
    is_leader = my_mp == 0

    width = inner // CUTS
    firsts = []
    for c in range(CUTS):
        cols = pl.ds(c * width, width)
        for i, (src, dst) in enumerate(((u_hbm, u_ref), (xp_hbm, xp_ref))):
            firsts.append(pltpu.make_async_copy(src.at[:, cols], dst.at[:, cols],
                                                cut_sem.at[c, i]))
    loads = [pltpu.make_async_copy(src, dst, in_sem.at[i]) for i, (src, dst) in enumerate((
        (alog_hbm, alog_ref), (dtp_hbm, dtp_ref), (bias_hbm, bias_ref), (g_hbm, g_ref),
        (skip_hbm, skip_ref)))]
    for load in firsts + loads:
        load.start()

    barrier = pltpu.get_barrier_semaphore()

    @pl.when(is_leader)
    def _():
        for m in range(1, mp):
            pl.semaphore_signal(barrier, inc=1, device_id={"mp": m}, device_id_type=MESH)

    @pl.when(my_mp > 0)
    def _():
        pl.semaphore_wait(barrier, 1)
        pl.semaphore_signal(here, inc=1, device_id={"mp": 0}, device_id_type=MESH)
        if mp > 2:
            pl.semaphore_wait(here, 1)

    @pl.when(is_leader)
    def _():
        pl.semaphore_wait(here, mp - 1)
        if mp > 2:
            for m in range(1, mp):
                pl.semaphore_signal(here, inc=1, device_id={"mp": m}, device_id_type=MESH)

        @pl.when(is_owner)
        def _():
            @pl.loop(1, group)
            def _(p):
                pl.semaphore_signal(barrier, inc=1,
                                    device_id={"seq": base + lax.rem(mine + p, group)},
                                    device_id_type=MESH)
            if groups > 1:
                @pl.loop(0, my_group)
                def _(g):
                    pl.semaphore_signal(barrier, inc=1, device_id={"seq": g * group + mine},
                                        device_id_type=MESH)

    def meet():
        @pl.when(is_leader)
        def _():
            @pl.when(is_owner)
            def _():
                pl.semaphore_wait(barrier, OWNERS - 1 + (groups - 1 - my_group))

            @pl.when(jnp.logical_not(is_owner))
            def _():
                pl.semaphore_wait(barrier, OWNERS)
            for m in range(1, mp):
                pl.semaphore_signal(ready, inc=1, device_id={"mp": m}, device_id_type=MESH)

        @pl.when(my_mp > 0)
        def _():
            pl.semaphore_wait(ready, 1)

    part = None
    for c in range(CUTS):
        firsts[2 * c].wait()
        firsts[2 * c + 1].wait()
        cols = slice(c * width, (c + 1) * width)
        term = lax.dot_general(u_ref[:, cols], xp_ref[:, cols], (((1,), (1,)), ((), ())),
                               preferred_element_type=F32)
        part = term if part is None else part + term
    proj[my_mp] = part
    shares = []
    for m in range(1, mp):
        copy = pltpu.make_async_remote_copy(
            src_ref=proj.at[my_mp], dst_ref=proj.at[my_mp],
            send_sem=mp_send.at[m - 1], recv_sem=mp_recv.at[m - 1],
            device_id={"mp": lax.rem(my_mp + m, mp)},
            device_id_type=MESH)
        copy.start()
        shares.append(copy)

    for load in loads[:3]:
        load.wait()
    for b in range(blocks):
        rate[b] = jnp.exp(alog_ref[:, b * LANES:(b + 1) * LANES]) * (-LOG2E)

    for copy in shares:
        copy.wait()
    whole = proj[0]
    for m in range(1, mp):
        whole = whole + proj[m]
    low = whole[:, :rank].astype(BF16)

    def columns(b):
        return at(b * LANES, LANES)

    def steps():
        for q in range(blocks // WAYS):
            raw = jnp.dot(low, dtp_ref[:, q * WAYS * LANES:(q + 1) * WAYS * LANES],
                          preferred_element_type=F32)
            for i in range(WAYS):
                b = q * WAYS + i
                cols = slice(b * LANES, (b + 1) * LANES)
                dt = softplus(raw[:, i * LANES:(i + 1) * LANES] + bias_ref[:, cols])
                dts[b] = dt
                drv[b] = dt * u_ref[:, cols].astype(F32)
                sums[b % OWNERS, b // OWNERS] = jnp.sum(dt, axis=0, keepdims=True)

    def spread():
        turned = whole[:, rank:rank + states].T
        for t in range(tokens):
            bl[t * states:(t + 1) * states, :] = jnp.broadcast_to(
                turned[:, t:t + 1], (states, LANES))

    def place():
        lane = lax.broadcasted_iota(jnp.int32, (whole.shape[1], SPAN * states), 1)
        line = lax.broadcasted_iota(jnp.int32, (whole.shape[1], SPAN * states), 0)
        pick = jnp.where(line == rank + states + lax.rem(lane, states), 1.0, 0.0).astype(BF16)
        wide = jnp.dot(whole.astype(BF16), pick, preferred_element_type=F32)
        lane = lax.broadcasted_iota(jnp.int32, wide.shape, 1)
        line = lax.broadcasted_iota(jnp.int32, wide.shape, 0)
        cbd[...] = jnp.where(lane // states == lax.rem(line, SPAN), wide, 0.0).astype(BF16)

    def share_sums():
        @pl.when(is_owner)
        def _():
            got_s[mine] = sums[row]
        for r, spot in enumerate(SPOTS):
            @pl.when(mine != spot)
            def _(r=r, spot=spot):
                pltpu.make_async_remote_copy(
                    src_ref=sums.at[r], dst_ref=got_s.at[mine], send_sem=s_send, recv_sem=s_recv,
                    device_id={"seq": base + spot}, device_id_type=MESH).start()

    def ends(q):
        ours = range(q * WAYS, (q + 1) * WAYS)
        rates = [[rate[b, v * half:(v + 1) * half, :] for v in range(2)] for b in ours]

        def body(it, hs):
            hs = list(hs)
            for i in range(SPAN):
                t = it * SPAN + i
                bb = [bl[at(t * states + v * half, half), :] for v in range(2)]
                for w, b in enumerate(ours):
                    dt = dts[b, pl.ds(t, 1), :]
                    dr = drv[b, pl.ds(t, 1), :]
                    for v in range(2):
                        fade = jnp.exp2(rates[w][v] * dt)
                        hs[2 * w + v] = fade * hs[2 * w + v] + bb[v] * dr
                        hist[b, at(t * states + v * half, half), :] = hs[2 * w + v]
            return tuple(hs)

        zero = jnp.zeros((half, LANES), F32)
        final = lax.fori_loop(0, tokens // SPAN, body, (zero,) * (2 * WAYS))
        for w, b in enumerate(ours):
            for v in range(2):
                tot[b, v * half:(v + 1) * half, :] = final[2 * w + v]

    def sends_end():
        return jnp.logical_or(mine != last, groups > 1)

    def share_ends(q):
        for b in range(q * WAYS, (q + 1) * WAYS):
            spot = SPOTS[b % OWNERS]

            @pl.when(mine == spot)
            def _(b=b):
                got_e[b // OWNERS, mine] = tot[b]

            @pl.when(jnp.logical_and(mine != spot, sends_end()))
            def _(b=b, spot=spot):
                pltpu.make_async_remote_copy(
                    src_ref=tot.at[b], dst_ref=got_e.at[b // OWNERS, mine],
                    send_sem=e_send.at[b], recv_sem=e_recv.at[b // OWNERS, mine],
                    device_id={"seq": base + spot}, device_id_type=MESH).start()

    def weigh(ours, scale):
        for g in range(tokens // SPAN):
            here_t = slice(g * SPAN, (g + 1) * SPAN)
            past = slice(g * SPAN * states, (g + 1) * SPAN * states)
            if scale is None:
                h = jnp.concatenate([hist[b, past, :].astype(BF16) for b in ours], axis=1)
            else:
                h = jnp.concatenate([gone[b, past, :] * scale[w] for w, b in enumerate(ours)],
                                    axis=1)
            y = jnp.dot(cbd[here_t, :], h, preferred_element_type=F32)
            for w, b in enumerate(ours):
                term = y[:, w * LANES:(w + 1) * LANES]
                ys[b, here_t, :] = term if scale is None else ys[b, here_t, :] + term

    def totals(ours):
        line = lax.broadcasted_iota(jnp.int32, (tokens, 2 * tokens), 0)
        lane = lax.broadcasted_iota(jnp.int32, (tokens, 2 * tokens), 1)
        upto = jnp.where(lax.rem(lane, tokens) <= line, 1.0, 0.0).astype(BF16)
        dt = jnp.concatenate([dts[b] for b in ours], axis=1)
        most = dt.astype(BF16)
        rest = (dt - most.astype(F32)).astype(BF16)
        total = jnp.dot(upto, jnp.concatenate([most, rest], axis=0), preferred_element_type=F32)
        for w, b in enumerate(ours):
            dts[b] = total[:, w * LANES:(w + 1) * LANES]

    def fade(ours):
        rates = [rate[b] for b in ours]

        @pl.loop(0, tokens // SPAN)
        def _(it):
            for i in range(SPAN):
                t = it * SPAN + i
                for w, b in enumerate(ours):
                    gone[b, at(t * states, states), :] = jnp.exp2(
                        rates[w] * dts[b, pl.ds(t, 1), :]).astype(BF16)

    def drain(part, sem):
        pltpu.make_async_copy(part, part, sem).wait()

    def arrived(k, j):
        @pl.when(j != mine)
        def _():
            drain(got_e.at[k, j], e_recv.at[k, j])

    def own(k):
        has = jnp.logical_and(is_owner, k * OWNERS + row < blocks)

        if k == 0:
            @pl.when(is_owner)
            def _():
                drain(got_s.at[pl.ds(0, group - 1)], s_recv)

        @pl.when(has)
        def _():
            rt = rate[k * OWNERS + row]
            fades = [jnp.exp2(rt * got_s[j, k]) for j in range(group)]
            carry = jnp.zeros((states, LANES), F32)
            if groups > 1:
                end, span = carry, carry
                for j in range(group):
                    arrived(k, j)
                    end = fades[j] * end + got_e[k, j]
                    span = span + got_s[j, k]
                near[k, 0] = end
                near[k, 1] = span

                @pl.loop(my_group + 1, groups)
                def _(g):
                    pltpu.make_async_remote_copy(
                        src_ref=near.at[k], dst_ref=far.at[k, my_group],
                        send_sem=f_send.at[k, g], recv_sem=f_recv.at[k, my_group],
                        device_id={"seq": g * group + mine}, device_id_type=MESH).start()

                @pl.loop(my_group + 1, groups)
                def _(g):
                    drain(near.at[k], f_send.at[k, g])

                def follow(g, carry):
                    drain(far.at[k, g], f_recv.at[k, g])
                    return jnp.exp2(rt * far[k, g, 1]) * carry + far[k, g, 0]
                carry = lax.fori_loop(0, my_group, follow, carry)
            for j in range(group):
                if j > 0 or groups > 1:
                    @pl.when(j == mine)
                    def _(carry=carry):
                        ent[k * OWNERS + row] = carry

                    @pl.when(j != mine)
                    def _(carry=carry, j=j):
                        back[k, j] = carry
                        pltpu.make_async_remote_copy(
                            src_ref=back.at[k, j], dst_ref=ent.at[k * OWNERS + row],
                            send_sem=b_send.at[k], recv_sem=b_recv.at[k * OWNERS + row],
                            device_id={"seq": base + j}, device_id_type=MESH).start()
                if j < last:
                    if groups == 1:
                        arrived(k, j)
                    carry = fades[j] * carry + got_e[k, j]

    def correct(ours):
        @pl.when(jnp.logical_or(mine > 0, groups > 1))
        def _():
            for b in ours:
                @pl.when(mine != SPOTS[b % OWNERS])
                def _(b=b):
                    drain(ent.at[b], b_recv.at[b])
            weigh(ours, [jnp.tile(ent[b].astype(BF16), (SPAN, 1)) for b in ours])

    def finish(ours):
        @pl.loop(ours[0], ours[-1] + 1)
        def _(b):
            cols = columns(b)
            g = g_ref[:, cols].astype(F32)
            mixed = (ys[b] + skip_ref[:, cols] * u_ref[:, cols].astype(F32)) * (
                g / (1.0 + jnp.exp(-g)))
            out_ref[:, cols] = mixed.astype(out_ref.dtype)

    chunks = [range(lo, min(lo + OWNERS, blocks)) for lo in range(0, blocks, OWNERS)]
    pieces = chunks[:-1] + [range(lo, lo + WAYS) for lo in range(chunks[-1][0], blocks, WAYS)]
    if blocks % OWNERS:
        for r in range(blocks % OWNERS, OWNERS):
            sums[r, rounds - 1] = jnp.zeros((1, LANES), F32)
    steps()
    spread()
    for q in range(blocks // WAYS):
        ends(q)
        if q == 0:
            meet()
            share_sums()
        share_ends(q)
    place()
    for ours in chunks:
        weigh(ours, None)
    for k, ours in enumerate(chunks):
        own(k)
        totals(ours)
        fade(ours)
    loads[3].wait()
    loads[4].wait()
    for ours in pieces:
        correct(ours)
        finish(ours)

    @pl.when(is_owner)
    def _():
        drain(sums.at[pl.ds(0, OWNERS - 1)], s_send)

    @pl.when(jnp.logical_not(is_owner))
    def _():
        drain(sums, s_send)
    for b in range(blocks):
        @pl.when(jnp.logical_and(mine != SPOTS[b % OWNERS], sends_end()))
        def _(b=b):
            drain(tot.at[b], e_send.at[b])
    for k in range(rounds):
        @pl.when(jnp.logical_and(is_owner, k * OWNERS + row < blocks))
        def _(k=k):
            drain(back.at[k, pl.ds(0, group - 1 if groups > 1 else group - 2)], b_send.at[k])


def solution(mesh):
    seq, mp = mesh.shape["seq"], mesh.shape["mp"]

    def per_device(inner_act, gate_act, x_proj, dt_proj, dt_bias, a_log, skip):
        tokens, inner = inner_act.shape
        rank, states = dt_proj.shape[0], a_log.shape[0]
        blocks = inner // LANES
        rounds = pl.cdiv(blocks, OWNERS)
        group = len(SPOTS) * 2
        groups = seq // group
        hbm = pl.BlockSpec(memory_space=pltpu.MemorySpace.HBM)
        args = tuple(pltpu.with_memory_space_constraint(a, pltpu.HBM) for a in (
            inner_act, gate_act, x_proj.T, dt_proj, dt_bias.reshape(1, inner), a_log,
            skip.reshape(1, inner)))
        cell = (states, LANES)
        dma = pltpu.SemaphoreType.DMA
        return pl.pallas_call(
            functools.partial(kernel, seq, mp, tokens, inner, rank, states),
            out_shape=pltpu.VMEM((tokens, inner), jnp.bfloat16),
            in_specs=[hbm] * len(args),
            out_specs=pl.BlockSpec(memory_space=pltpu.VMEM),
            scratch_shapes=[pltpu.VMEM(a.shape, a.dtype) for a in args] + [
                pltpu.VMEM((mp, tokens, x_proj.shape[1]), F32),
                pltpu.VMEM((tokens * states, LANES), F32),
                pltpu.VMEM((tokens, SPAN * states), BF16),
                pltpu.VMEM((blocks,) + cell, F32),
                pltpu.VMEM((blocks, tokens, LANES), F32),
                pltpu.VMEM((blocks, tokens, LANES), F32),
                pltpu.VMEM((blocks, tokens, LANES), F32),
                pltpu.VMEM((blocks, tokens * states, LANES), F32),
                pltpu.VMEM((blocks, tokens * states, LANES), BF16),
                pltpu.VMEM((blocks,) + cell, F32),
                pltpu.VMEM((OWNERS, rounds, 1, LANES), F32),
                pltpu.VMEM((rounds, group) + cell, F32),
                pltpu.VMEM((group, rounds, 1, LANES), F32),
                pltpu.VMEM((rounds, group) + cell, F32),
                pltpu.VMEM((blocks,) + cell, F32),
                pltpu.VMEM((rounds, groups, 2) + cell, F32),
                pltpu.VMEM((rounds, 2) + cell, F32),
                dma((5,)), dma((CUTS, 2)),
                dma((mp - 1,)), dma((mp - 1,)),
                dma((blocks,)), dma((rounds, group)),
                dma, dma,
                dma((rounds,)), dma((blocks,)),
                dma((rounds, groups)), dma((rounds, groups)),
                pltpu.SemaphoreType.REGULAR, pltpu.SemaphoreType.REGULAR,
            ],
            compiler_params=pltpu.CompilerParams(
                collective_id=0, has_side_effects=True,
                vmem_limit_bytes=58 * 1024 * 1024),
        )(*args)

    placed = (
        P("seq", "mp"),
        P("seq", "mp"),
        P("mp", None),
        P(None, "mp"),
        P("mp"),
        P(None, "mp"),
        P("mp"),
    )
    return jax.shard_map(
        per_device, mesh=mesh, in_specs=placed, out_specs=P("seq", "mp"), check_vma=False
    )
```

```python
import functools

import jax
import jax.numpy as jnp
from jax import lax
from jax.experimental import pallas as pl
from jax.experimental.pallas import tpu as pltpu
from jax.sharding import PartitionSpec as P

LANES = 128
OWNERS = 8
SPOTS = (4, 11, 5, 10, 6, 9, 7, 8)
WAYS = 4
SPAN = 16
CUTS = 4
LOG2E = 1.4426950408889634
F32 = jnp.float32
BF16 = jnp.bfloat16
MESH = pl.DeviceIdType.MESH


def softplus(x):
    e = jnp.exp(-jnp.abs(x))
    series = e * (1.0 - e * (0.5 - e * (1.0 / 3.0 - e * (0.25 - e * 0.2))))
    return jnp.maximum(x, 0.0) + jnp.where(e < 0.03125, series, jnp.log(1.0 + e))


def at(start, size):
    return pl.ds(pl.multiple_of(start, size), size)


def kernel(seq, mp, tokens, inner, rank, states,
           u_hbm, g_hbm, xp_hbm, dtp_hbm, bias_hbm, alog_hbm, skip_hbm, out_ref,
           u_ref, g_ref, xp_ref, dtp_ref, bias_ref, alog_ref, skip_ref,
           proj, bl, cbd, rate, dts, drv, ys, hist, gone, tot, sums, got_e, got_s, back, ent,
           far, near, in_sem, cut_sem, mp_send, mp_recv, e_send, e_recv, s_send, s_recv, b_send,
           b_recv, f_send, f_recv, here, ready):
    blocks = inner // LANES
    rounds = pl.cdiv(blocks, OWNERS)
    group = len(SPOTS) * 2
    groups = seq // group
    last = group - 1
    half = states // 2
    me = lax.axis_index("seq")
    my_mp = lax.axis_index("mp")
    mine = lax.rem(me, group)
    my_group = me // group
    base = my_group * group
    row = sum(jnp.where(mine == spot, r, 0) for r, spot in enumerate(SPOTS))
    is_owner = jnp.logical_and(mine >= min(SPOTS), mine <= max(SPOTS))
    is_leader = my_mp == 0

    width = inner // CUTS
    firsts = []
    for c in range(CUTS):
        cols = pl.ds(c * width, width)
        for i, (src, dst) in enumerate(((u_hbm, u_ref), (xp_hbm, xp_ref))):
            firsts.append(pltpu.make_async_copy(src.at[:, cols], dst.at[:, cols],
                                                cut_sem.at[c, i]))
    loads = [pltpu.make_async_copy(src, dst, in_sem.at[i]) for i, (src, dst) in enumerate((
        (alog_hbm, alog_ref), (dtp_hbm, dtp_ref), (bias_hbm, bias_ref), (g_hbm, g_ref),
        (skip_hbm, skip_ref)))]
    for load in firsts + loads:
        load.start()

    barrier = pltpu.get_barrier_semaphore()

    @pl.when(is_leader)
    def _():
        for m in range(1, mp):
            pl.semaphore_signal(barrier, inc=1, device_id={"mp": m}, device_id_type=MESH)

    @pl.when(my_mp > 0)
    def _():
        pl.semaphore_wait(barrier, 1)
        pl.semaphore_signal(here, inc=1, device_id={"mp": 0}, device_id_type=MESH)
        if mp > 2:
            pl.semaphore_wait(here, 1)

    @pl.when(is_leader)
    def _():
        pl.semaphore_wait(here, mp - 1)
        if mp > 2:
            for m in range(1, mp):
                pl.semaphore_signal(here, inc=1, device_id={"mp": m}, device_id_type=MESH)

        @pl.when(is_owner)
        def _():
            @pl.loop(1, group)
            def _(p):
                pl.semaphore_signal(barrier, inc=1,
                                    device_id={"seq": base + lax.rem(mine + p, group)},
                                    device_id_type=MESH)
            if groups > 1:
                @pl.loop(0, my_group)
                def _(g):
                    pl.semaphore_signal(barrier, inc=1, device_id={"seq": g * group + mine},
                                        device_id_type=MESH)

    def meet():
        @pl.when(is_leader)
        def _():
            @pl.when(is_owner)
            def _():
                pl.semaphore_wait(barrier, OWNERS - 1 + (groups - 1 - my_group))

            @pl.when(jnp.logical_not(is_owner))
            def _():
                pl.semaphore_wait(barrier, OWNERS)
            for m in range(1, mp):
                pl.semaphore_signal(ready, inc=1, device_id={"mp": m}, device_id_type=MESH)

        @pl.when(my_mp > 0)
        def _():
            pl.semaphore_wait(ready, 1)

    part = None
    for c in range(CUTS):
        firsts[2 * c].wait()
        firsts[2 * c + 1].wait()
        cols = slice(c * width, (c + 1) * width)
        term = lax.dot_general(u_ref[:, cols], xp_ref[:, cols], (((1,), (1,)), ((), ())),
                               preferred_element_type=F32)
        part = term if part is None else part + term
    proj[my_mp] = part
    shares = []
    for m in range(1, mp):
        copy = pltpu.make_async_remote_copy(
            src_ref=proj.at[my_mp], dst_ref=proj.at[my_mp],
            send_sem=mp_send.at[m - 1], recv_sem=mp_recv.at[m - 1],
            device_id={"mp": lax.rem(my_mp + m, mp)},
            device_id_type=MESH)
        copy.start()
        shares.append(copy)

    for load in loads[:3]:
        load.wait()
    for b in range(blocks):
        rate[b] = jnp.exp(alog_ref[:, b * LANES:(b + 1) * LANES]) * (-LOG2E)

    for copy in shares:
        copy.wait()
    whole = proj[0]
    for m in range(1, mp):
        whole = whole + proj[m]
    low = whole[:, :rank].astype(BF16)

    chunks = [range(lo, min(lo + OWNERS, blocks)) for lo in range(0, blocks, OWNERS)]
    pieces = chunks[:-1] + [range(lo, lo + WAYS) for lo in range(chunks[-1][0], blocks, WAYS)]

    def columns(b):
        return at(b * LANES, LANES)

    def steps():
        for q in range(blocks // WAYS):
            raw = jnp.dot(low, dtp_ref[:, q * WAYS * LANES:(q + 1) * WAYS * LANES],
                          preferred_element_type=F32)
            for i in range(WAYS):
                b = q * WAYS + i
                cols = slice(b * LANES, (b + 1) * LANES)
                dt = softplus(raw[:, i * LANES:(i + 1) * LANES] + bias_ref[:, cols])
                dts[b] = dt
                drv[b] = dt * u_ref[:, cols].astype(F32)
                sums[b % OWNERS, b // OWNERS] = jnp.sum(dt, axis=0, keepdims=True)

    def spread():
        turned = whole[:, rank:rank + states].T
        for t in range(tokens):
            bl[t * states:(t + 1) * states, :] = jnp.broadcast_to(
                turned[:, t:t + 1], (states, LANES))

    def place():
        lane = lax.broadcasted_iota(jnp.int32, (whole.shape[1], SPAN * states), 1)
        line = lax.broadcasted_iota(jnp.int32, (whole.shape[1], SPAN * states), 0)
        pick = jnp.where(line == rank + states + lax.rem(lane, states), 1.0, 0.0).astype(BF16)
        wide = jnp.dot(whole.astype(BF16), pick, preferred_element_type=F32)
        lane = lax.broadcasted_iota(jnp.int32, wide.shape, 1)
        line = lax.broadcasted_iota(jnp.int32, wide.shape, 0)
        cbd[...] = jnp.where(lane // states == lax.rem(line, SPAN), wide, 0.0).astype(BF16)

    def share_sums():
        @pl.when(is_owner)
        def _():
            got_s[mine] = sums[row]
        for r, spot in enumerate(SPOTS):
            @pl.when(mine != spot)
            def _(r=r, spot=spot):
                pltpu.make_async_remote_copy(
                    src_ref=sums.at[r], dst_ref=got_s.at[mine], send_sem=s_send, recv_sem=s_recv,
                    device_id={"seq": base + spot}, device_id_type=MESH).start()

    def ends(q):
        ours = range(q * WAYS, (q + 1) * WAYS)
        rates = [[rate[b, v * half:(v + 1) * half, :] for v in range(2)] for b in ours]

        def body(it, hs):
            hs = list(hs)
            for i in range(SPAN):
                t = it * SPAN + i
                bb = [bl[at(t * states + v * half, half), :] for v in range(2)]
                for w, b in enumerate(ours):
                    dt = dts[b, pl.ds(t, 1), :]
                    dr = drv[b, pl.ds(t, 1), :]
                    for v in range(2):
                        fade = jnp.exp2(rates[w][v] * dt)
                        hs[2 * w + v] = fade * hs[2 * w + v] + bb[v] * dr
                        hist[b, at(t * states + v * half, half), :] = hs[2 * w + v]
            return tuple(hs)

        zero = jnp.zeros((half, LANES), F32)
        final = lax.fori_loop(0, tokens // SPAN, body, (zero,) * (2 * WAYS))
        for w, b in enumerate(ours):
            for v in range(2):
                tot[b, v * half:(v + 1) * half, :] = final[2 * w + v]

    def sends_end():
        return jnp.logical_or(mine != last, groups > 1)

    def share_ends(q):
        @pl.when(sends_end())
        def _():
            for b in range(q * WAYS, (q + 1) * WAYS):
                spot = SPOTS[b % OWNERS]

                @pl.when(mine != spot)
                def _(b=b, spot=spot):
                    pltpu.make_async_remote_copy(
                        src_ref=tot.at[b], dst_ref=got_e.at[b // OWNERS, mine],
                        send_sem=e_send.at[b // OWNERS], recv_sem=e_recv.at[b // OWNERS, mine],
                        device_id={"seq": base + spot}, device_id_type=MESH).start()

    def weigh(ours, scale):
        for g in range(tokens // SPAN):
            here_t = slice(g * SPAN, (g + 1) * SPAN)
            past = slice(g * SPAN * states, (g + 1) * SPAN * states)
            if scale is None:
                h = jnp.concatenate([hist[b, past, :].astype(BF16) for b in ours], axis=1)
            else:
                h = jnp.concatenate([gone[b, past, :] * scale[w] for w, b in enumerate(ours)],
                                    axis=1)
            y = jnp.dot(cbd[here_t, :], h, preferred_element_type=F32)
            for w, b in enumerate(ours):
                term = y[:, w * LANES:(w + 1) * LANES]
                ys[b, here_t, :] = term if scale is None else ys[b, here_t, :] + term

    def totals(ours):
        line = lax.broadcasted_iota(jnp.int32, (tokens, 2 * tokens), 0)
        lane = lax.broadcasted_iota(jnp.int32, (tokens, 2 * tokens), 1)
        upto = jnp.where(lax.rem(lane, tokens) <= line, 1.0, 0.0).astype(BF16)
        dt = jnp.concatenate([dts[b] for b in ours], axis=1)
        most = dt.astype(BF16)
        rest = (dt - most.astype(F32)).astype(BF16)
        total = jnp.dot(upto, jnp.concatenate([most, rest], axis=0), preferred_element_type=F32)
        for w, b in enumerate(ours):
            dts[b] = total[:, w * LANES:(w + 1) * LANES]

    def fade(ours):
        rates = [rate[b] for b in ours]

        @pl.loop(0, tokens // SPAN)
        def _(it):
            for i in range(SPAN):
                t = it * SPAN + i
                for w, b in enumerate(ours):
                    gone[b, at(t * states, states), :] = jnp.exp2(
                        rates[w] * dts[b, pl.ds(t, 1), :]).astype(BF16)

    def drain(part, sem):
        pltpu.make_async_copy(part, part, sem).wait()

    def others(lo, hi, act):
        pl.loop(lo, jnp.clip(mine, lo, hi))(act)
        pl.loop(jnp.clip(mine + 1, lo, hi), hi)(act)

    def holds(ours):
        return jnp.logical_and(is_owner, jnp.logical_and(
            row >= ours[0] % OWNERS, row <= ours[-1] % OWNERS))

    def all_but_own(ref, ours, sem):
        @pl.when(holds(ours))
        def _():
            drain(ref.at[pl.ds(ours[0], len(ours) - 1)], sem)

        @pl.when(jnp.logical_not(holds(ours)))
        def _():
            drain(ref.at[pl.ds(ours[0], len(ours))], sem)

    def own(k, part):
        size = group // 2
        lo, hi = part * size, (part + 1) * size
        block = k * OWNERS + row
        piece = k if k < rounds - 1 else k + row // WAYS

        if k == 0 and part == 0:
            @pl.when(is_owner)
            def _():
                drain(got_s.at[pl.ds(0, group - 1)], s_recv)

        @pl.when(holds(chunks[k]))
        def _():
            rt = rate[block]
            fades = [jnp.exp2(rt * got_s[j, k]) for j in range(max(lo - 1, 0), hi - 1)]
            if part == 0:
                got_e[k, mine] = tot[block]
            if groups == 1:
                others(max(lo - 1, 0), hi - 1, lambda j: drain(got_e.at[k, j], e_recv.at[k, j]))
            carry = jnp.zeros((states, LANES), F32)
            if groups > 1 and part == 0:
                others(0, group, lambda j: drain(got_e.at[k, j], e_recv.at[k, j]))
                end, span = carry, carry
                for j in range(group):
                    end = jnp.exp2(rt * got_s[j, k]) * end + got_e[k, j]
                    span = span + got_s[j, k]
                near[k, 0] = end
                near[k, 1] = span

                @pl.loop(my_group + 1, groups)
                def _(g):
                    pltpu.make_async_remote_copy(
                        src_ref=near.at[k], dst_ref=far.at[k, my_group],
                        send_sem=f_send.at[k, g], recv_sem=f_recv.at[k, my_group],
                        device_id={"seq": g * group + mine}, device_id_type=MESH).start()

                @pl.loop(my_group + 1, groups)
                def _(g):
                    drain(near.at[k], f_send.at[k, g])

                def follow(g, carry):
                    drain(far.at[k, g], f_recv.at[k, g])
                    return jnp.exp2(rt * far[k, g, 1]) * carry + far[k, g, 0]
                carry = lax.fori_loop(0, my_group, follow, carry)
            for j in range(lo, hi):
                if j > 0:
                    before = back[k, j - 1] if j == lo else carry
                    carry = fades[j - 1 - max(lo - 1, 0)] * before + got_e[k, j - 1]
                back[k, j] = carry

            @pl.when(jnp.logical_and(mine >= lo, mine < hi))
            def _():
                ent[block] = back[k, mine]

            def give(j):
                pltpu.make_async_remote_copy(
                    src_ref=back.at[k, j], dst_ref=ent.at[block],
                    send_sem=b_send.at[k], recv_sem=b_recv.at[piece],
                    device_id={"seq": base + j}, device_id_type=MESH).start()
            others(1 if part == 0 and groups == 1 else lo, hi, give)

    def correct(n, ours):
        @pl.when(jnp.logical_or(mine > 0, groups > 1))
        def _():
            all_but_own(ent, ours, b_recv.at[n])
            weigh(ours, [jnp.tile(ent[b].astype(BF16), (SPAN, 1)) for b in ours])

    def finish(ours):
        @pl.loop(ours[0], ours[-1] + 1)
        def _(b):
            cols = columns(b)
            g = g_ref[:, cols].astype(F32)
            mixed = (ys[b] + skip_ref[:, cols] * u_ref[:, cols].astype(F32)) * (
                g / (1.0 + jnp.exp(-g)))
            out_ref[:, cols] = mixed.astype(out_ref.dtype)

    if blocks % OWNERS:
        for r in range(blocks % OWNERS, OWNERS):
            sums[r, rounds - 1] = jnp.zeros((1, LANES), F32)
    steps()
    spread()
    for q in range(blocks // WAYS):
        ends(q)
        if q == 0:
            meet()
            share_sums()
        share_ends(q)
    place()
    for ours in chunks:
        weigh(ours, None)
    turns = [(k, part) for k in range(rounds) for part in range(2)]
    turns = turns[:1] + [t for i in range(1, len(turns) - 1, 2) for t in (turns[i:i + 2],)] + [
        turns[-1:]]
    turns[0] = [turns[0]]
    for q in range(blocks // WAYS):
        ours = range(q * WAYS, (q + 1) * WAYS)
        totals(ours)
        fade(ours)
        if q < len(turns):
            for k, part in turns[q]:
                own(k, part)
    loads[3].wait()
    loads[4].wait()
    for n, ours in enumerate(pieces):
        correct(n, ours)
        finish(ours)

    @pl.when(is_owner)
    def _():
        drain(sums.at[pl.ds(0, OWNERS - 1)], s_send)

    @pl.when(jnp.logical_not(is_owner))
    def _():
        drain(sums, s_send)
    @pl.when(sends_end())
    def _():
        for k, ours in enumerate(chunks):
            all_but_own(tot, ours, e_send.at[k])
    for k in range(rounds):
        @pl.when(holds(chunks[k]))
        def _(k=k):
            drain(back.at[k, pl.ds(0, group - 1 if groups > 1 else group - 2)], b_send.at[k])


def solution(mesh):
    seq, mp = mesh.shape["seq"], mesh.shape["mp"]

    def per_device(inner_act, gate_act, x_proj, dt_proj, dt_bias, a_log, skip):
        tokens, inner = inner_act.shape
        rank, states = dt_proj.shape[0], a_log.shape[0]
        blocks = inner // LANES
        rounds = pl.cdiv(blocks, OWNERS)
        group = len(SPOTS) * 2
        groups = seq // group
        hbm = pl.BlockSpec(memory_space=pltpu.MemorySpace.HBM)
        args = tuple(pltpu.with_memory_space_constraint(a, pltpu.HBM) for a in (
            inner_act, gate_act, x_proj.T, dt_proj, dt_bias.reshape(1, inner), a_log,
            skip.reshape(1, inner)))
        cell = (states, LANES)
        dma = pltpu.SemaphoreType.DMA
        return pl.pallas_call(
            functools.partial(kernel, seq, mp, tokens, inner, rank, states),
            out_shape=pltpu.VMEM((tokens, inner), jnp.bfloat16),
            in_specs=[hbm] * len(args),
            out_specs=pl.BlockSpec(memory_space=pltpu.VMEM),
            scratch_shapes=[pltpu.VMEM(a.shape, a.dtype) for a in args] + [
                pltpu.VMEM((mp, tokens, x_proj.shape[1]), F32),
                pltpu.VMEM((tokens * states, LANES), F32),
                pltpu.VMEM((tokens, SPAN * states), BF16),
                pltpu.VMEM((blocks,) + cell, F32),
                pltpu.VMEM((blocks, tokens, LANES), F32),
                pltpu.VMEM((blocks, tokens, LANES), F32),
                pltpu.VMEM((blocks, tokens, LANES), F32),
                pltpu.VMEM((blocks, tokens * states, LANES), F32),
                pltpu.VMEM((blocks, tokens * states, LANES), BF16),
                pltpu.VMEM((blocks,) + cell, F32),
                pltpu.VMEM((OWNERS, rounds, 1, LANES), F32),
                pltpu.VMEM((rounds, group) + cell, F32),
                pltpu.VMEM((group, rounds, 1, LANES), F32),
                pltpu.VMEM((rounds, group) + cell, F32),
                pltpu.VMEM((blocks,) + cell, F32),
                pltpu.VMEM((rounds, groups, 2) + cell, F32),
                pltpu.VMEM((rounds, 2) + cell, F32),
                dma((5,)), dma((CUTS, 2)),
                dma((mp - 1,)), dma((mp - 1,)),
                dma((rounds,)), dma((rounds, group)),
                dma, dma,
                dma((rounds,)), dma((rounds + 1,)),
                dma((rounds, groups)), dma((rounds, groups)),
                pltpu.SemaphoreType.REGULAR, pltpu.SemaphoreType.REGULAR,
            ],
            compiler_params=pltpu.CompilerParams(
                collective_id=0, has_side_effects=True,
                vmem_limit_bytes=58 * 1024 * 1024),
        )(*args)

    placed = (
        P("seq", "mp"),
        P("seq", "mp"),
        P("mp", None),
        P(None, "mp"),
        P("mp"),
        P(None, "mp"),
        P("mp"),
    )
    return jax.shard_map(
        per_device, mesh=mesh, in_specs=placed, out_specs=P("seq", "mp"), check_vma=False
    )
```

```python
import functools

import jax
import jax.numpy as jnp
from jax import lax
from jax.experimental import pallas as pl
from jax.experimental.pallas import tpu as pltpu
from jax.sharding import PartitionSpec as P

LANES = 128
OWNERS = 8
SPOTS = (4, 11, 5, 10, 6, 9, 7, 8)
WAYS = 4
SPAN = 16
CUTS = 4
LOG2E = 1.4426950408889634
F32 = jnp.float32
BF16 = jnp.bfloat16
MESH = pl.DeviceIdType.MESH


def softplus(x):
    e = jnp.exp(-jnp.abs(x))
    series = e * (1.0 - e * (0.5 - e * (1.0 / 3.0 - e * (0.25 - e * 0.2))))
    return jnp.maximum(x, 0.0) + jnp.where(e < 0.03125, series, jnp.log(1.0 + e))


def at(start, size):
    return pl.ds(pl.multiple_of(start, size), size)


def kernel(seq, mp, tokens, inner, rank, states,
           u_hbm, g_hbm, xp_hbm, dtp_hbm, bias_hbm, alog_hbm, skip_hbm, out_ref,
           u_ref, g_ref, xp_ref, dtp_ref, bias_ref, alog_ref, skip_ref,
           proj, bl, cbd, rate, dts, drv, ys, hist, gone, tot, sums, got_e, got_s, back, ent,
           far, near, in_sem, cut_sem, mp_send, mp_recv, e_send, e_recv, s_send, s_recv, b_send,
           b_recv, f_send, f_recv, here, ready):
    blocks = inner // LANES
    rounds = pl.cdiv(blocks, OWNERS)
    group = len(SPOTS) * 2
    groups = seq // group
    last = group - 1
    half = states // 2
    me = lax.axis_index("seq")
    my_mp = lax.axis_index("mp")
    mine = lax.rem(me, group)
    my_group = me // group
    base = my_group * group
    row = sum(jnp.where(mine == spot, r, 0) for r, spot in enumerate(SPOTS))
    is_owner = jnp.logical_and(mine >= min(SPOTS), mine <= max(SPOTS))
    is_leader = my_mp == 0

    width = inner // CUTS
    firsts = []
    for c in range(CUTS):
        cols = pl.ds(c * width, width)
        for i, (src, dst) in enumerate(((u_hbm, u_ref), (xp_hbm, xp_ref))):
            firsts.append(pltpu.make_async_copy(src.at[:, cols], dst.at[:, cols],
                                                cut_sem.at[c, i]))
    loads = [pltpu.make_async_copy(src, dst, in_sem.at[i]) for i, (src, dst) in enumerate((
        (alog_hbm, alog_ref), (dtp_hbm, dtp_ref), (bias_hbm, bias_ref), (g_hbm, g_ref),
        (skip_hbm, skip_ref)))]
    for load in firsts + loads:
        load.start()

    barrier = pltpu.get_barrier_semaphore()

    @pl.when(is_leader)
    def _():
        for m in range(1, mp):
            pl.semaphore_signal(barrier, inc=1, device_id={"mp": m}, device_id_type=MESH)

    @pl.when(my_mp > 0)
    def _():
        pl.semaphore_wait(barrier, 1)
        pl.semaphore_signal(here, inc=1, device_id={"mp": 0}, device_id_type=MESH)
        if mp > 2:
            pl.semaphore_wait(here, 1)

    @pl.when(is_leader)
    def _():
        pl.semaphore_wait(here, mp - 1)
        if mp > 2:
            for m in range(1, mp):
                pl.semaphore_signal(here, inc=1, device_id={"mp": m}, device_id_type=MESH)

        @pl.when(is_owner)
        def _():
            @pl.loop(1, group)
            def _(p):
                pl.semaphore_signal(barrier, inc=1,
                                    device_id={"seq": base + lax.rem(mine + p, group)},
                                    device_id_type=MESH)
            if groups > 1:
                @pl.loop(0, my_group)
                def _(g):
                    pl.semaphore_signal(barrier, inc=1, device_id={"seq": g * group + mine},
                                        device_id_type=MESH)

    def meet():
        @pl.when(is_leader)
        def _():
            @pl.when(is_owner)
            def _():
                pl.semaphore_wait(barrier, OWNERS - 1 + (groups - 1 - my_group))

            @pl.when(jnp.logical_not(is_owner))
            def _():
                pl.semaphore_wait(barrier, OWNERS)
            for m in range(1, mp):
                pl.semaphore_signal(ready, inc=1, device_id={"mp": m}, device_id_type=MESH)

        @pl.when(my_mp > 0)
        def _():
            pl.semaphore_wait(ready, 1)

    part = None
    for c in range(CUTS):
        firsts[2 * c].wait()
        firsts[2 * c + 1].wait()
        cols = slice(c * width, (c + 1) * width)
        term = lax.dot_general(u_ref[:, cols], xp_ref[:, cols], (((1,), (1,)), ((), ())),
                               preferred_element_type=F32)
        part = term if part is None else part + term
    proj[my_mp] = part
    shares = []
    for m in range(1, mp):
        copy = pltpu.make_async_remote_copy(
            src_ref=proj.at[my_mp], dst_ref=proj.at[my_mp],
            send_sem=mp_send.at[m - 1], recv_sem=mp_recv.at[m - 1],
            device_id={"mp": lax.rem(my_mp + m, mp)},
            device_id_type=MESH)
        copy.start()
        shares.append(copy)

    for load in loads[:3]:
        load.wait()
    for b in range(blocks):
        rate[b] = jnp.exp(alog_ref[:, b * LANES:(b + 1) * LANES]) * (-LOG2E)

    for copy in shares:
        copy.wait()
    whole = proj[0]
    for m in range(1, mp):
        whole = whole + proj[m]
    low = whole[:, :rank].astype(BF16)

    chunks = [range(lo, min(lo + OWNERS, blocks)) for lo in range(0, blocks, OWNERS)]
    pieces = chunks[:-1] + [range(lo, lo + WAYS) for lo in range(chunks[-1][0], blocks, WAYS)]

    def columns(b):
        return at(b * LANES, LANES)

    def steps():
        for q in range(blocks // WAYS):
            raw = jnp.dot(low, dtp_ref[:, q * WAYS * LANES:(q + 1) * WAYS * LANES],
                          preferred_element_type=F32)
            for i in range(WAYS):
                b = q * WAYS + i
                cols = slice(b * LANES, (b + 1) * LANES)
                dt = softplus(raw[:, i * LANES:(i + 1) * LANES] + bias_ref[:, cols])
                dts[b] = dt
                drv[b] = dt * u_ref[:, cols].astype(F32)
                sums[b % OWNERS, b // OWNERS] = jnp.sum(dt, axis=0, keepdims=True)

    def spread():
        turned = whole[:, rank:rank + states].T
        for t in range(tokens):
            bl[t * states:(t + 1) * states, :] = jnp.broadcast_to(
                turned[:, t:t + 1], (states, LANES))

    def place():
        lane = lax.broadcasted_iota(jnp.int32, (whole.shape[1], SPAN * states), 1)
        line = lax.broadcasted_iota(jnp.int32, (whole.shape[1], SPAN * states), 0)
        pick = jnp.where(line == rank + states + lax.rem(lane, states), 1.0, 0.0).astype(BF16)
        wide = jnp.dot(whole.astype(BF16), pick, preferred_element_type=F32)
        lane = lax.broadcasted_iota(jnp.int32, wide.shape, 1)
        line = lax.broadcasted_iota(jnp.int32, wide.shape, 0)
        cbd[...] = jnp.where(lane // states == lax.rem(line, SPAN), wide, 0.0).astype(BF16)

    def share_sums():
        @pl.when(is_owner)
        def _():
            got_s[mine] = sums[row]
        for r, spot in enumerate(SPOTS):
            @pl.when(mine != spot)
            def _(r=r, spot=spot):
                pltpu.make_async_remote_copy(
                    src_ref=sums.at[r], dst_ref=got_s.at[mine], send_sem=s_send, recv_sem=s_recv,
                    device_id={"seq": base + spot}, device_id_type=MESH).start()

    def ends(q):
        ours = range(q * WAYS, (q + 1) * WAYS)
        rates = [[rate[b, v * half:(v + 1) * half, :] for v in range(2)] for b in ours]

        def body(it, hs):
            hs = list(hs)
            for i in range(SPAN):
                t = it * SPAN + i
                bb = [bl[at(t * states + v * half, half), :] for v in range(2)]
                for w, b in enumerate(ours):
                    dt = dts[b, pl.ds(t, 1), :]
                    dr = drv[b, pl.ds(t, 1), :]
                    for v in range(2):
                        fade = jnp.exp2(rates[w][v] * dt)
                        hs[2 * w + v] = fade * hs[2 * w + v] + bb[v] * dr
                        hist[b, at(t * states + v * half, half), :] = hs[2 * w + v]
            return tuple(hs)

        zero = jnp.zeros((half, LANES), F32)
        final = lax.fori_loop(0, tokens // SPAN, body, (zero,) * (2 * WAYS))
        for w, b in enumerate(ours):
            for v in range(2):
                tot[b, v * half:(v + 1) * half, :] = final[2 * w + v]

    def sends_end():
        return jnp.logical_or(mine != last, groups > 1)

    def share_ends(q):
        @pl.when(sends_end())
        def _():
            for b in range(q * WAYS, (q + 1) * WAYS):
                spot = SPOTS[b % OWNERS]

                @pl.when(mine != spot)
                def _(b=b, spot=spot):
                    pltpu.make_async_remote_copy(
                        src_ref=tot.at[b], dst_ref=got_e.at[b // OWNERS, mine],
                        send_sem=e_send.at[b // OWNERS], recv_sem=e_recv.at[b // OWNERS, mine],
                        device_id={"seq": base + spot}, device_id_type=MESH).start()

    def weigh(ours):
        entered = [jnp.tile(ent[b].astype(BF16), (SPAN, 1)) for b in ours]
        for g in range(tokens // SPAN):
            here_t = slice(g * SPAN, (g + 1) * SPAN)
            past = slice(g * SPAN * states, (g + 1) * SPAN * states)
            h = jnp.concatenate([gone[b, past, :] * entered[w] for w, b in enumerate(ours)],
                                axis=1)
            y = jnp.dot(cbd[here_t, :], h, preferred_element_type=F32)
            for w, b in enumerate(ours):
                ys[b, here_t, :] = ys[b, here_t, :] + y[:, w * LANES:(w + 1) * LANES]

    def totals(ours):
        line = lax.broadcasted_iota(jnp.int32, (tokens, 2 * tokens), 0)
        lane = lax.broadcasted_iota(jnp.int32, (tokens, 2 * tokens), 1)
        upto = jnp.where(lax.rem(lane, tokens) <= line, 1.0, 0.0).astype(BF16)
        dt = jnp.concatenate([dts[b] for b in ours], axis=1)
        most = dt.astype(BF16)
        rest = (dt - most.astype(F32)).astype(BF16)
        total = jnp.dot(upto, jnp.concatenate([most, rest], axis=0), preferred_element_type=F32)
        for w, b in enumerate(ours):
            dts[b] = total[:, w * LANES:(w + 1) * LANES]

    def fade(ours):
        rates = [rate[b] for b in ours]
        each = OWNERS // len(ours)

        @pl.loop(0, tokens // (SPAN * each))
        def _(it):
            rows = [it * each + e for e in range(each)]
            sums_of = []
            for g in rows:
                past = at(g * (SPAN * states), SPAN * states)
                h = jnp.concatenate([hist[b, past, :].astype(BF16) for b in ours], axis=1)
                sums_of.append(jnp.dot(cbd[at(g * SPAN, SPAN), :], h,
                                       preferred_element_type=F32))
            for i in range(SPAN * each):
                t = it * (SPAN * each) + i
                for w, b in enumerate(ours):
                    gone[b, at(t * states, states), :] = jnp.exp2(
                        rates[w] * dts[b, pl.ds(t, 1), :]).astype(BF16)
            for g, y in zip(rows, sums_of):
                for w, b in enumerate(ours):
                    ys[b, at(g * SPAN, SPAN), :] = y[:, w * LANES:(w + 1) * LANES]

    def drain(part, sem):
        pltpu.make_async_copy(part, part, sem).wait()

    def others(lo, hi, act):
        pl.loop(lo, jnp.clip(mine, lo, hi))(act)
        pl.loop(jnp.clip(mine + 1, lo, hi), hi)(act)

    def holds(ours):
        return jnp.logical_and(is_owner, jnp.logical_and(
            row >= ours[0] % OWNERS, row <= ours[-1] % OWNERS))

    def all_but_own(ref, ours, sem):
        @pl.when(holds(ours))
        def _():
            drain(ref.at[pl.ds(ours[0], len(ours) - 1)], sem)

        @pl.when(jnp.logical_not(holds(ours)))
        def _():
            drain(ref.at[pl.ds(ours[0], len(ours))], sem)

    def own(k, part):
        size = group // 2
        lo, hi = part * size, (part + 1) * size
        block = k * OWNERS + row
        piece = k if k < rounds - 1 else k + row // WAYS

        if k == 0 and part == 0:
            @pl.when(is_owner)
            def _():
                drain(got_s.at[pl.ds(0, group - 1)], s_recv)

        @pl.when(holds(chunks[k]))
        def _():
            rt = rate[block]
            fades = [jnp.exp2(rt * got_s[j, k]) for j in range(max(lo - 1, 0), hi - 1)]
            if part == 0:
                got_e[k, mine] = tot[block]
            if groups == 1:
                others(max(lo - 1, 0), hi - 1, lambda j: drain(got_e.at[k, j], e_recv.at[k, j]))
            carry = jnp.zeros((states, LANES), F32)
            if groups > 1 and part == 0:
                others(0, group, lambda j: drain(got_e.at[k, j], e_recv.at[k, j]))
                end, span = carry, carry
                for j in range(group):
                    end = jnp.exp2(rt * got_s[j, k]) * end + got_e[k, j]
                    span = span + got_s[j, k]
                near[k, 0] = end
                near[k, 1] = span

                @pl.loop(my_group + 1, groups)
                def _(g):
                    pltpu.make_async_remote_copy(
                        src_ref=near.at[k], dst_ref=far.at[k, my_group],
                        send_sem=f_send.at[k, g], recv_sem=f_recv.at[k, my_group],
                        device_id={"seq": g * group + mine}, device_id_type=MESH).start()

                @pl.loop(my_group + 1, groups)
                def _(g):
                    drain(near.at[k], f_send.at[k, g])

                def follow(g, carry):
                    drain(far.at[k, g], f_recv.at[k, g])
                    return jnp.exp2(rt * far[k, g, 1]) * carry + far[k, g, 0]
                carry = lax.fori_loop(0, my_group, follow, carry)
            for j in range(lo, hi):
                if j > 0:
                    before = back[k, j - 1] if j == lo else carry
                    carry = fades[j - 1 - max(lo - 1, 0)] * before + got_e[k, j - 1]
                back[k, j] = carry

            @pl.when(jnp.logical_and(mine >= lo, mine < hi))
            def _():
                ent[block] = back[k, mine]

            def give(j):
                pltpu.make_async_remote_copy(
                    src_ref=back.at[k, j], dst_ref=ent.at[block],
                    send_sem=b_send.at[k], recv_sem=b_recv.at[piece],
                    device_id={"seq": base + j}, device_id_type=MESH).start()
            others(1 if part == 0 and groups == 1 else lo, hi, give)

    def correct(n, ours):
        @pl.when(jnp.logical_or(mine > 0, groups > 1))
        def _():
            all_but_own(ent, ours, b_recv.at[n])
            weigh(ours)

    def finish(ours):
        @pl.loop(ours[0], ours[-1] + 1)
        def _(b):
            cols = columns(b)
            g = g_ref[:, cols].astype(F32)
            mixed = (ys[b] + skip_ref[:, cols] * u_ref[:, cols].astype(F32)) * (
                0.5 * g * (1.0 + jnp.tanh(0.5 * g)))
            out_ref[:, cols] = mixed.astype(out_ref.dtype)

    if blocks % OWNERS:
        for r in range(blocks % OWNERS, OWNERS):
            sums[r, rounds - 1] = jnp.zeros((1, LANES), F32)
    steps()
    spread()
    for q in range(blocks // WAYS):
        ends(q)
        if q == 0:
            meet()
            share_sums()
        share_ends(q)
    place()
    turns = [(k, part) for k in range(rounds) for part in range(2)]
    turns = turns[:1] + [t for i in range(1, len(turns) - 1, 2) for t in (turns[i:i + 2],)] + [
        turns[-1:]]
    turns[0] = [turns[0]]
    for q in range(blocks // WAYS):
        ours = range(q * WAYS, (q + 1) * WAYS)
        totals(ours)
        fade(ours)
        if q < len(turns):
            for k, part in turns[q]:
                own(k, part)
    loads[3].wait()
    loads[4].wait()
    for n, ours in enumerate(pieces):
        correct(n, ours)
        finish(ours)

    @pl.when(is_owner)
    def _():
        drain(sums.at[pl.ds(0, OWNERS - 1)], s_send)

    @pl.when(jnp.logical_not(is_owner))
    def _():
        drain(sums, s_send)
    @pl.when(sends_end())
    def _():
        for k, ours in enumerate(chunks):
            all_but_own(tot, ours, e_send.at[k])
    for k in range(rounds):
        @pl.when(holds(chunks[k]))
        def _(k=k):
            drain(back.at[k, pl.ds(0, group - 1 if groups > 1 else group - 2)], b_send.at[k])


def solution(mesh):
    seq, mp = mesh.shape["seq"], mesh.shape["mp"]

    def per_device(inner_act, gate_act, x_proj, dt_proj, dt_bias, a_log, skip):
        tokens, inner = inner_act.shape
        rank, states = dt_proj.shape[0], a_log.shape[0]
        blocks = inner // LANES
        rounds = pl.cdiv(blocks, OWNERS)
        group = len(SPOTS) * 2
        groups = seq // group
        hbm = pl.BlockSpec(memory_space=pltpu.MemorySpace.HBM)
        args = tuple(pltpu.with_memory_space_constraint(a, pltpu.HBM) for a in (
            inner_act, gate_act, x_proj.T, dt_proj, dt_bias.reshape(1, inner), a_log,
            skip.reshape(1, inner)))
        cell = (states, LANES)
        dma = pltpu.SemaphoreType.DMA
        return pl.pallas_call(
            functools.partial(kernel, seq, mp, tokens, inner, rank, states),
            out_shape=pltpu.VMEM((tokens, inner), jnp.bfloat16),
            in_specs=[hbm] * len(args),
            out_specs=pl.BlockSpec(memory_space=pltpu.VMEM),
            scratch_shapes=[pltpu.VMEM(a.shape, a.dtype) for a in args] + [
                pltpu.VMEM((mp, tokens, x_proj.shape[1]), F32),
                pltpu.VMEM((tokens * states, LANES), F32),
                pltpu.VMEM((tokens, SPAN * states), BF16),
                pltpu.VMEM((blocks,) + cell, F32),
                pltpu.VMEM((blocks, tokens, LANES), F32),
                pltpu.VMEM((blocks, tokens, LANES), F32),
                pltpu.VMEM((blocks, tokens, LANES), F32),
                pltpu.VMEM((blocks, tokens * states, LANES), F32),
                pltpu.VMEM((blocks, tokens * states, LANES), BF16),
                pltpu.VMEM((blocks,) + cell, F32),
                pltpu.VMEM((OWNERS, rounds, 1, LANES), F32),
                pltpu.VMEM((rounds, group) + cell, F32),
                pltpu.VMEM((group, rounds, 1, LANES), F32),
                pltpu.VMEM((rounds, group) + cell, F32),
                pltpu.VMEM((blocks,) + cell, F32),
                pltpu.VMEM((rounds, groups, 2) + cell, F32),
                pltpu.VMEM((rounds, 2) + cell, F32),
                dma((5,)), dma((CUTS, 2)),
                dma((mp - 1,)), dma((mp - 1,)),
                dma((rounds,)), dma((rounds, group)),
                dma, dma,
                dma((rounds,)), dma((rounds + 1,)),
                dma((rounds, groups)), dma((rounds, groups)),
                pltpu.SemaphoreType.REGULAR, pltpu.SemaphoreType.REGULAR,
            ],
            compiler_params=pltpu.CompilerParams(
                collective_id=0, has_side_effects=True,
                vmem_limit_bytes=58 * 1024 * 1024),
        )(*args)

    placed = (
        P("seq", "mp"),
        P("seq", "mp"),
        P("mp", None),
        P(None, "mp"),
        P("mp"),
        P(None, "mp"),
        P("mp"),
    )
    return jax.shard_map(
        per_device, mesh=mesh, in_specs=placed, out_specs=P("seq", "mp"), check_vma=False
    )
```

```python
import functools

import jax
import jax.numpy as jnp
from jax import lax
from jax.experimental import pallas as pl
from jax.experimental.pallas import tpu as pltpu
from jax.sharding import PartitionSpec as P

LANES = 128
OWNERS = 8
SPOTS = (4, 11, 5, 10, 6, 9, 7, 8)
WAYS = 4
SPAN = 16
CUTS = 4
LOG2E = 1.4426950408889634
F32 = jnp.float32
BF16 = jnp.bfloat16
MESH = pl.DeviceIdType.MESH


def softplus(x):
    e = jnp.exp(-jnp.abs(x))
    series = e * (1.0 - e * (0.5 - e * (1.0 / 3.0 - e * (0.25 - e * 0.2))))
    return jnp.maximum(x, 0.0) + jnp.where(e < 0.03125, series, jnp.log(1.0 + e))


def at(start, size):
    return pl.ds(pl.multiple_of(start, size), size)


def kernel(seq, mp, tokens, inner, rank, states,
           u_hbm, g_hbm, xp_hbm, dtp_hbm, bias_hbm, alog_hbm, skip_hbm, out_ref,
           u_ref, g_ref, xp_ref, dtp_ref, bias_ref, alog_ref, skip_ref,
           proj, bl, cbd, rate, dts, drv, ys, hist, gone, tot, sums, got_e, got_s, back, ent,
           far, near, in_sem, cut_sem, mp_send, mp_recv, e_send, e_recv, s_send, s_recv, b_send,
           b_recv, f_send, f_recv, here, ready):
    blocks = inner // LANES
    rounds = pl.cdiv(blocks, OWNERS)
    group = len(SPOTS) * 2
    groups = seq // group
    last = group - 1
    half = states // 2
    me = lax.axis_index("seq")
    my_mp = lax.axis_index("mp")
    mine = lax.rem(me, group)
    my_group = me // group
    base = my_group * group
    row = sum(jnp.where(mine == spot, r, 0) for r, spot in enumerate(SPOTS))
    is_owner = jnp.logical_and(mine >= min(SPOTS), mine <= max(SPOTS))
    is_leader = my_mp == 0

    width = inner // CUTS
    firsts = []
    for c in range(CUTS):
        cols = pl.ds(c * width, width)
        for i, (src, dst) in enumerate(((u_hbm, u_ref), (xp_hbm, xp_ref))):
            firsts.append(pltpu.make_async_copy(src.at[:, cols], dst.at[:, cols],
                                                cut_sem.at[c, i]))
    loads = [pltpu.make_async_copy(src, dst, in_sem.at[i]) for i, (src, dst) in enumerate((
        (alog_hbm, alog_ref), (dtp_hbm, dtp_ref), (bias_hbm, bias_ref), (g_hbm, g_ref),
        (skip_hbm, skip_ref)))]
    for load in firsts + loads[:3]:
        load.start()

    barrier = pltpu.get_barrier_semaphore()

    @pl.when(is_leader)
    def _():
        for m in range(1, mp):
            pl.semaphore_signal(barrier, inc=1, device_id={"mp": m}, device_id_type=MESH)

    @pl.when(my_mp > 0)
    def _():
        pl.semaphore_wait(barrier, 1)
        pl.semaphore_signal(here, inc=1, device_id={"mp": 0}, device_id_type=MESH)
        if mp > 2:
            pl.semaphore_wait(here, 1)

    @pl.when(is_leader)
    def _():
        pl.semaphore_wait(here, mp - 1)
        if mp > 2:
            for m in range(1, mp):
                pl.semaphore_signal(here, inc=1, device_id={"mp": m}, device_id_type=MESH)

        @pl.when(is_owner)
        def _():
            @pl.loop(1, group)
            def _(p):
                pl.semaphore_signal(barrier, inc=1,
                                    device_id={"seq": base + lax.rem(mine + p, group)},
                                    device_id_type=MESH)
            if groups > 1:
                @pl.loop(0, my_group)
                def _(g):
                    pl.semaphore_signal(barrier, inc=1, device_id={"seq": g * group + mine},
                                        device_id_type=MESH)

    def meet():
        @pl.when(is_leader)
        def _():
            @pl.when(is_owner)
            def _():
                pl.semaphore_wait(barrier, OWNERS - 1 + (groups - 1 - my_group))

            @pl.when(jnp.logical_not(is_owner))
            def _():
                pl.semaphore_wait(barrier, OWNERS)
            for m in range(1, mp):
                pl.semaphore_signal(ready, inc=1, device_id={"mp": m}, device_id_type=MESH)

        @pl.when(my_mp > 0)
        def _():
            pl.semaphore_wait(ready, 1)

    part = None
    for c in range(CUTS):
        firsts[2 * c].wait()
        firsts[2 * c + 1].wait()
        cols = slice(c * width, (c + 1) * width)
        term = lax.dot_general(u_ref[:, cols], xp_ref[:, cols], (((1,), (1,)), ((), ())),
                               preferred_element_type=F32)
        part = term if part is None else part + term
    proj[my_mp] = part
    shares = []
    for m in range(1, mp):
        copy = pltpu.make_async_remote_copy(
            src_ref=proj.at[my_mp], dst_ref=proj.at[my_mp],
            send_sem=mp_send.at[m - 1], recv_sem=mp_recv.at[m - 1],
            device_id={"mp": lax.rem(my_mp + m, mp)},
            device_id_type=MESH)
        copy.start()
        shares.append(copy)

    for load in loads[3:]:
        load.start()
    for load in loads[:3]:
        load.wait()
    for b in range(blocks):
        rate[b] = jnp.exp(alog_ref[:, b * LANES:(b + 1) * LANES]) * (-LOG2E)

    for copy in shares:
        copy.wait()
    whole = proj[0]
    for m in range(1, mp):
        whole = whole + proj[m]
    low = whole[:, :rank].astype(BF16)

    chunks = [range(lo, min(lo + OWNERS, blocks)) for lo in range(0, blocks, OWNERS)]
    pieces = chunks[:-1] + [range(lo, lo + WAYS) for lo in range(chunks[-1][0], blocks, WAYS)]

    def columns(b):
        return at(b * LANES, LANES)

    def steps():
        for q in range(blocks // WAYS):
            raw = jnp.dot(low, dtp_ref[:, q * WAYS * LANES:(q + 1) * WAYS * LANES],
                          preferred_element_type=F32)
            for i in range(WAYS):
                b = q * WAYS + i
                cols = slice(b * LANES, (b + 1) * LANES)
                dt = softplus(raw[:, i * LANES:(i + 1) * LANES] + bias_ref[:, cols])
                dts[b] = dt
                drv[b] = dt * u_ref[:, cols].astype(F32)
                sums[b % OWNERS, b // OWNERS] = jnp.sum(dt, axis=0, keepdims=True)

    def spread():
        turned = whole[:, rank:rank + states].T
        for t in range(tokens):
            bl[t * states:(t + 1) * states, :] = jnp.broadcast_to(
                turned[:, t:t + 1], (states, LANES))

    def place():
        lane = lax.broadcasted_iota(jnp.int32, (whole.shape[1], SPAN * states), 1)
        line = lax.broadcasted_iota(jnp.int32, (whole.shape[1], SPAN * states), 0)
        pick = jnp.where(line == rank + states + lax.rem(lane, states), 1.0, 0.0).astype(BF16)
        wide = jnp.dot(whole.astype(BF16), pick, preferred_element_type=F32)
        lane = lax.broadcasted_iota(jnp.int32, wide.shape, 1)
        line = lax.broadcasted_iota(jnp.int32, wide.shape, 0)
        cbd[...] = jnp.where(lane // states == lax.rem(line, SPAN), wide, 0.0).astype(BF16)

    def share_sums():
        @pl.when(is_owner)
        def _():
            got_s[mine] = sums[row]
        for r, spot in enumerate(SPOTS):
            @pl.when(mine != spot)
            def _(r=r, spot=spot):
                pltpu.make_async_remote_copy(
                    src_ref=sums.at[r], dst_ref=got_s.at[mine], send_sem=s_send, recv_sem=s_recv,
                    device_id={"seq": base + spot}, device_id_type=MESH).start()

    def ends(q):
        ours = range(q * WAYS, (q + 1) * WAYS)
        rates = [[rate[b, v * half:(v + 1) * half, :] for v in range(2)] for b in ours]

        def body(it, hs):
            hs = list(hs)
            for i in range(SPAN):
                t = it * SPAN + i
                bb = [bl[at(t * states + v * half, half), :] for v in range(2)]
                for w, b in enumerate(ours):
                    dt = dts[b, pl.ds(t, 1), :]
                    dr = drv[b, pl.ds(t, 1), :]
                    for v in range(2):
                        fade = jnp.exp2(rates[w][v] * dt)
                        hs[2 * w + v] = fade * hs[2 * w + v] + bb[v] * dr
                        hist[b, at(t * states + v * half, half), :] = hs[2 * w + v]
            return tuple(hs)

        zero = jnp.zeros((half, LANES), F32)
        final = lax.fori_loop(0, tokens // SPAN, body, (zero,) * (2 * WAYS))
        for w, b in enumerate(ours):
            for v in range(2):
                tot[b, v * half:(v + 1) * half, :] = final[2 * w + v]

    def sends_end():
        return jnp.logical_or(mine != last, groups > 1)

    def share_ends(q):
        @pl.when(sends_end())
        def _():
            for b in range(q * WAYS, (q + 1) * WAYS):
                spot = SPOTS[b % OWNERS]

                @pl.when(mine != spot)
                def _(b=b, spot=spot):
                    pltpu.make_async_remote_copy(
                        src_ref=tot.at[b], dst_ref=got_e.at[b // OWNERS, mine],
                        send_sem=e_send.at[b // OWNERS], recv_sem=e_recv.at[b // OWNERS, mine],
                        device_id={"seq": base + spot}, device_id_type=MESH).start()

    def weigh(ours):
        entered = [jnp.tile(ent[b].astype(BF16), (SPAN, 1)) for b in ours]
        for g in range(tokens // SPAN):
            here_t = slice(g * SPAN, (g + 1) * SPAN)
            past = slice(g * SPAN * states, (g + 1) * SPAN * states)
            h = jnp.concatenate([gone[b, past, :] * entered[w] for w, b in enumerate(ours)],
                                axis=1)
            y = jnp.dot(cbd[here_t, :], h, preferred_element_type=F32)
            for w, b in enumerate(ours):
                ys[b, here_t, :] = ys[b, here_t, :] + y[:, w * LANES:(w + 1) * LANES]

    def totals(ours):
        line = lax.broadcasted_iota(jnp.int32, (tokens, 2 * tokens), 0)
        lane = lax.broadcasted_iota(jnp.int32, (tokens, 2 * tokens), 1)
        upto = jnp.where(lax.rem(lane, tokens) <= line, 1.0, 0.0).astype(BF16)
        dt = jnp.concatenate([dts[b] for b in ours], axis=1)
        most = dt.astype(BF16)
        rest = (dt - most.astype(F32)).astype(BF16)
        total = jnp.dot(upto, jnp.concatenate([most, rest], axis=0), preferred_element_type=F32)
        for w, b in enumerate(ours):
            dts[b] = total[:, w * LANES:(w + 1) * LANES]

    def fade(ours):
        rates = [rate[b] for b in ours]
        each = OWNERS // len(ours)

        @pl.loop(0, tokens // (SPAN * each))
        def _(it):
            rows = [it * each + e for e in range(each)]
            sums_of = []
            for g in rows:
                past = at(g * (SPAN * states), SPAN * states)
                h = jnp.concatenate([hist[b, past, :].astype(BF16) for b in ours], axis=1)
                sums_of.append(jnp.dot(cbd[at(g * SPAN, SPAN), :], h,
                                       preferred_element_type=F32))
            for i in range(SPAN * each):
                t = it * (SPAN * each) + i
                for w, b in enumerate(ours):
                    gone[b, at(t * states, states), :] = jnp.exp2(
                        rates[w] * dts[b, pl.ds(t, 1), :]).astype(BF16)
            for g, y in zip(rows, sums_of):
                for w, b in enumerate(ours):
                    ys[b, at(g * SPAN, SPAN), :] = y[:, w * LANES:(w + 1) * LANES]

    def drain(part, sem):
        pltpu.make_async_copy(part, part, sem).wait()

    def others(lo, hi, act):
        pl.loop(lo, jnp.clip(mine, lo, hi))(act)
        pl.loop(jnp.clip(mine + 1, lo, hi), hi)(act)

    def holds(ours):
        return jnp.logical_and(is_owner, jnp.logical_and(
            row >= ours[0] % OWNERS, row <= ours[-1] % OWNERS))

    def all_but_own(ref, ours, sem):
        @pl.when(holds(ours))
        def _():
            drain(ref.at[pl.ds(ours[0], len(ours) - 1)], sem)

        @pl.when(jnp.logical_not(holds(ours)))
        def _():
            drain(ref.at[pl.ds(ours[0], len(ours))], sem)

    def own(k, part):
        size = group // 2
        lo, hi = part * size, (part + 1) * size
        block = k * OWNERS + row
        piece = k if k < rounds - 1 else k + row // WAYS

        if k == 0 and part == 0:
            @pl.when(is_owner)
            def _():
                drain(got_s.at[pl.ds(0, group - 1)], s_recv)

        @pl.when(holds(chunks[k]))
        def _():
            rt = rate[block]
            fades = [jnp.exp2(rt * got_s[j, k]) for j in range(max(lo - 1, 0), hi - 1)]
            if part == 0:
                got_e[k, mine] = tot[block]
            if groups == 1:
                others(max(lo - 1, 0), hi - 1, lambda j: drain(got_e.at[k, j], e_recv.at[k, j]))
            carry = jnp.zeros((states, LANES), F32)
            if groups > 1 and part == 0:
                others(0, group, lambda j: drain(got_e.at[k, j], e_recv.at[k, j]))
                end, span = carry, carry
                for j in range(group):
                    end = jnp.exp2(rt * got_s[j, k]) * end + got_e[k, j]
                    span = span + got_s[j, k]
                near[k, 0] = end
                near[k, 1] = span

                @pl.loop(my_group + 1, groups)
                def _(g):
                    pltpu.make_async_remote_copy(
                        src_ref=near.at[k], dst_ref=far.at[k, my_group],
                        send_sem=f_send.at[k, g], recv_sem=f_recv.at[k, my_group],
                        device_id={"seq": g * group + mine}, device_id_type=MESH).start()

                @pl.loop(my_group + 1, groups)
                def _(g):
                    drain(near.at[k], f_send.at[k, g])

                def follow(g, carry):
                    drain(far.at[k, g], f_recv.at[k, g])
                    return jnp.exp2(rt * far[k, g, 1]) * carry + far[k, g, 0]
                carry = lax.fori_loop(0, my_group, follow, carry)
            for j in range(lo, hi):
                if j > 0:
                    before = back[k, j - 1] if j == lo else carry
                    carry = fades[j - 1 - max(lo - 1, 0)] * before + got_e[k, j - 1]
                back[k, j] = carry

            @pl.when(jnp.logical_and(mine >= lo, mine < hi))
            def _():
                ent[block] = back[k, mine]

            def give(j):
                pltpu.make_async_remote_copy(
                    src_ref=back.at[k, j], dst_ref=ent.at[block],
                    send_sem=b_send.at[k], recv_sem=b_recv.at[piece],
                    device_id={"seq": base + j}, device_id_type=MESH).start()
            others(1 if part == 0 and groups == 1 else lo, hi, give)

    def correct(n, ours):
        @pl.when(jnp.logical_or(mine > 0, groups > 1))
        def _():
            all_but_own(ent, ours, b_recv.at[n])
            weigh(ours)

    def finish(ours):
        @pl.loop(ours[0], ours[-1] + 1)
        def _(b):
            cols = columns(b)
            g = g_ref[:, cols].astype(F32)
            mixed = (ys[b] + skip_ref[:, cols] * u_ref[:, cols].astype(F32)) * (
                0.5 * g * (1.0 + jnp.tanh(0.5 * g)))
            out_ref[:, cols] = mixed.astype(out_ref.dtype)

    if blocks % OWNERS:
        for r in range(blocks % OWNERS, OWNERS):
            sums[r, rounds - 1] = jnp.zeros((1, LANES), F32)
    steps()
    spread()
    for q in range(blocks // WAYS):
        ends(q)
        if q == 0:
            meet()
            share_sums()
        share_ends(q)
    place()
    turns = [(k, part) for k in range(rounds) for part in range(2)]
    turns = turns[:1] + [t for i in range(1, len(turns) - 1, 2) for t in (turns[i:i + 2],)] + [
        turns[-1:]]
    turns[0] = [turns[0]]
    for q in range(blocks // WAYS):
        ours = range(q * WAYS, (q + 1) * WAYS)
        totals(ours)
        fade(ours)
        if q < len(turns):
            for k, part in turns[q]:
                own(k, part)
    loads[3].wait()
    loads[4].wait()
    for n, ours in enumerate(pieces):
        correct(n, ours)
        finish(ours)

    @pl.when(is_owner)
    def _():
        drain(sums.at[pl.ds(0, OWNERS - 1)], s_send)

    @pl.when(jnp.logical_not(is_owner))
    def _():
        drain(sums, s_send)
    @pl.when(sends_end())
    def _():
        for k, ours in enumerate(chunks):
            all_but_own(tot, ours, e_send.at[k])
    for k in range(rounds):
        @pl.when(holds(chunks[k]))
        def _(k=k):
            drain(back.at[k, pl.ds(0, group - 1 if groups > 1 else group - 2)], b_send.at[k])


def solution(mesh):
    seq, mp = mesh.shape["seq"], mesh.shape["mp"]

    def per_device(inner_act, gate_act, x_proj, dt_proj, dt_bias, a_log, skip):
        tokens, inner = inner_act.shape
        rank, states = dt_proj.shape[0], a_log.shape[0]
        blocks = inner // LANES
        rounds = pl.cdiv(blocks, OWNERS)
        group = len(SPOTS) * 2
        groups = seq // group
        hbm = pl.BlockSpec(memory_space=pltpu.MemorySpace.HBM)
        args = tuple(pltpu.with_memory_space_constraint(a, pltpu.HBM) for a in (
            inner_act, gate_act, x_proj.T, dt_proj, dt_bias.reshape(1, inner), a_log,
            skip.reshape(1, inner)))
        cell = (states, LANES)
        dma = pltpu.SemaphoreType.DMA
        return pl.pallas_call(
            functools.partial(kernel, seq, mp, tokens, inner, rank, states),
            out_shape=pltpu.VMEM((tokens, inner), jnp.bfloat16),
            in_specs=[hbm] * len(args),
            out_specs=pl.BlockSpec(memory_space=pltpu.VMEM),
            scratch_shapes=[pltpu.VMEM(a.shape, a.dtype) for a in args] + [
                pltpu.VMEM((mp, tokens, x_proj.shape[1]), F32),
                pltpu.VMEM((tokens * states, LANES), F32),
                pltpu.VMEM((tokens, SPAN * states), BF16),
                pltpu.VMEM((blocks,) + cell, F32),
                pltpu.VMEM((blocks, tokens, LANES), F32),
                pltpu.VMEM((blocks, tokens, LANES), F32),
                pltpu.VMEM((blocks, tokens, LANES), F32),
                pltpu.VMEM((blocks, tokens * states, LANES), F32),
                pltpu.VMEM((blocks, tokens * states, LANES), BF16),
                pltpu.VMEM((blocks,) + cell, F32),
                pltpu.VMEM((OWNERS, rounds, 1, LANES), F32),
                pltpu.VMEM((rounds, group) + cell, F32),
                pltpu.VMEM((group, rounds, 1, LANES), F32),
                pltpu.VMEM((rounds, group) + cell, F32),
                pltpu.VMEM((blocks,) + cell, F32),
                pltpu.VMEM((rounds, groups, 2) + cell, F32),
                pltpu.VMEM((rounds, 2) + cell, F32),
                dma((5,)), dma((CUTS, 2)),
                dma((mp - 1,)), dma((mp - 1,)),
                dma((rounds,)), dma((rounds, group)),
                dma, dma,
                dma((rounds,)), dma((rounds + 1,)),
                dma((rounds, groups)), dma((rounds, groups)),
                pltpu.SemaphoreType.REGULAR, pltpu.SemaphoreType.REGULAR,
            ],
            compiler_params=pltpu.CompilerParams(
                collective_id=0, has_side_effects=True,
                vmem_limit_bytes=58 * 1024 * 1024),
        )(*args)

    placed = (
        P("seq", "mp"),
        P("seq", "mp"),
        P("mp", None),
        P(None, "mp"),
        P("mp"),
        P(None, "mp"),
        P("mp"),
    )
    return jax.shard_map(
        per_device, mesh=mesh, in_specs=placed, out_specs=P("seq", "mp"), check_vma=False
    )
```

```python
import functools

import jax
import jax.numpy as jnp
from jax import lax
from jax.experimental import pallas as pl
from jax.experimental.pallas import tpu as pltpu
from jax.sharding import PartitionSpec as P

LANES = 128
OWNERS = 8
SPOTS = (4, 11, 5, 10, 6, 9, 7, 8)
WAYS = 4
SPAN = 16
CUTS = 4
LOG2E = 1.4426950408889634
F32 = jnp.float32
BF16 = jnp.bfloat16
MESH = pl.DeviceIdType.MESH


def softplus(x):
    e = jnp.exp(-jnp.abs(x))
    series = e * (1.0 - e * (0.5 - e * (1.0 / 3.0 - e * (0.25 - e * 0.2))))
    return jnp.maximum(x, 0.0) + jnp.where(e < 0.03125, series, jnp.log(1.0 + e))


def at(start, size):
    return pl.ds(pl.multiple_of(start, size), size)


def kernel(seq, mp, tokens, inner, rank, states,
           u_hbm, g_hbm, xp_hbm, dtp_hbm, bias_hbm, alog_hbm, skip_hbm, out_ref,
           u_ref, g_ref, xp_ref, dtp_ref, bias_ref, alog_ref, skip_ref,
           proj, bl, cbd, rate, dts, drv, ys, hist, gone, tot, sums, got_e, got_s, back, ent,
           far, near, in_sem, cut_sem, mp_send, mp_recv, e_send, e_recv, s_send, s_recv, b_send,
           b_recv, f_send, f_recv, here, ready):
    blocks = inner // LANES
    rounds = pl.cdiv(blocks, OWNERS)
    group = len(SPOTS) * 2
    groups = seq // group
    last = group - 1
    half = states // 2
    me = lax.axis_index("seq")
    my_mp = lax.axis_index("mp")
    mine = lax.rem(me, group)
    my_group = me // group
    base = my_group * group
    row = sum(jnp.where(mine == spot, r, 0) for r, spot in enumerate(SPOTS))
    is_owner = jnp.logical_and(mine >= min(SPOTS), mine <= max(SPOTS))
    is_leader = my_mp == 0

    width = inner // CUTS
    firsts = []
    for c in range(CUTS):
        cols = pl.ds(c * width, width)
        for i, (src, dst) in enumerate(((u_hbm, u_ref), (xp_hbm, xp_ref))):
            firsts.append(pltpu.make_async_copy(src.at[:, cols], dst.at[:, cols],
                                                cut_sem.at[c, i]))
    loads = [pltpu.make_async_copy(src, dst, in_sem.at[i]) for i, (src, dst) in enumerate((
        (alog_hbm, alog_ref), (dtp_hbm, dtp_ref), (bias_hbm, bias_ref), (g_hbm, g_ref),
        (skip_hbm, skip_ref)))]
    for load in firsts:
        load.start()

    barrier = pltpu.get_barrier_semaphore()

    @pl.when(is_leader)
    def _():
        for m in range(1, mp):
            pl.semaphore_signal(barrier, inc=1, device_id={"mp": m}, device_id_type=MESH)

    @pl.when(my_mp > 0)
    def _():
        pl.semaphore_wait(barrier, 1)
        pl.semaphore_signal(here, inc=1, device_id={"mp": 0}, device_id_type=MESH)
        if mp > 2:
            pl.semaphore_wait(here, 1)

    @pl.when(is_leader)
    def _():
        pl.semaphore_wait(here, mp - 1)
        if mp > 2:
            for m in range(1, mp):
                pl.semaphore_signal(here, inc=1, device_id={"mp": m}, device_id_type=MESH)

        @pl.when(is_owner)
        def _():
            @pl.loop(1, group)
            def _(p):
                pl.semaphore_signal(barrier, inc=1,
                                    device_id={"seq": base + lax.rem(mine + p, group)},
                                    device_id_type=MESH)
            if groups > 1:
                @pl.loop(0, my_group)
                def _(g):
                    pl.semaphore_signal(barrier, inc=1, device_id={"seq": g * group + mine},
                                        device_id_type=MESH)

    def meet():
        @pl.when(is_leader)
        def _():
            @pl.when(is_owner)
            def _():
                pl.semaphore_wait(barrier, OWNERS - 1 + (groups - 1 - my_group))

            @pl.when(jnp.logical_not(is_owner))
            def _():
                pl.semaphore_wait(barrier, OWNERS)
            for m in range(1, mp):
                pl.semaphore_signal(ready, inc=1, device_id={"mp": m}, device_id_type=MESH)

        @pl.when(my_mp > 0)
        def _():
            pl.semaphore_wait(ready, 1)

    part = None
    for c in range(CUTS):
        firsts[2 * c].wait()
        firsts[2 * c + 1].wait()
        if c == CUTS // 2:
            for load in loads[:3]:
                load.start()
        cols = slice(c * width, (c + 1) * width)
        term = lax.dot_general(u_ref[:, cols], xp_ref[:, cols], (((1,), (1,)), ((), ())),
                               preferred_element_type=F32)
        part = term if part is None else part + term
    proj[my_mp] = part
    shares = []
    for m in range(1, mp):
        copy = pltpu.make_async_remote_copy(
            src_ref=proj.at[my_mp], dst_ref=proj.at[my_mp],
            send_sem=mp_send.at[m - 1], recv_sem=mp_recv.at[m - 1],
            device_id={"mp": lax.rem(my_mp + m, mp)},
            device_id_type=MESH)
        copy.start()
        shares.append(copy)

    for load in loads[3:]:
        load.start()
    for load in loads[:3]:
        load.wait()
    for b in range(blocks):
        rate[b] = jnp.exp(alog_ref[:, b * LANES:(b + 1) * LANES]) * (-LOG2E)

    for copy in shares:
        copy.wait()
    whole = proj[0]
    for m in range(1, mp):
        whole = whole + proj[m]
    low = whole[:, :rank].astype(BF16)

    chunks = [range(lo, min(lo + OWNERS, blocks)) for lo in range(0, blocks, OWNERS)]
    pieces = chunks[:-1] + [range(lo, lo + WAYS) for lo in range(chunks[-1][0], blocks, WAYS)]

    def columns(b):
        return at(b * LANES, LANES)

    def steps():
        for q in range(blocks // WAYS):
            raw = jnp.dot(low, dtp_ref[:, q * WAYS * LANES:(q + 1) * WAYS * LANES],
                          preferred_element_type=F32)
            for i in range(WAYS):
                b = q * WAYS + i
                cols = slice(b * LANES, (b + 1) * LANES)
                dt = softplus(raw[:, i * LANES:(i + 1) * LANES] + bias_ref[:, cols])
                dts[b] = dt
                drv[b] = dt * u_ref[:, cols].astype(F32)
                sums[b % OWNERS, b // OWNERS] = jnp.sum(dt, axis=0, keepdims=True)

    def spread():
        turned = whole[:, rank:rank + states].T
        for t in range(tokens):
            bl[t * states:(t + 1) * states, :] = jnp.broadcast_to(
                turned[:, t:t + 1], (states, LANES))

    def place():
        lane = lax.broadcasted_iota(jnp.int32, (whole.shape[1], SPAN * states), 1)
        line = lax.broadcasted_iota(jnp.int32, (whole.shape[1], SPAN * states), 0)
        pick = jnp.where(line == rank + states + lax.rem(lane, states), 1.0, 0.0).astype(BF16)
        wide = jnp.dot(whole.astype(BF16), pick, preferred_element_type=F32)
        lane = lax.broadcasted_iota(jnp.int32, wide.shape, 1)
        line = lax.broadcasted_iota(jnp.int32, wide.shape, 0)
        cbd[...] = jnp.where(lane // states == lax.rem(line, SPAN), wide, 0.0).astype(BF16)

    def share_sums():
        @pl.when(is_owner)
        def _():
            got_s[mine] = sums[row]
        for r, spot in enumerate(SPOTS):
            @pl.when(mine != spot)
            def _(r=r, spot=spot):
                pltpu.make_async_remote_copy(
                    src_ref=sums.at[r], dst_ref=got_s.at[mine], send_sem=s_send, recv_sem=s_recv,
                    device_id={"seq": base + spot}, device_id_type=MESH).start()

    def ends(q):
        ours = range(q * WAYS, (q + 1) * WAYS)
        rates = [[rate[b, v * half:(v + 1) * half, :] for v in range(2)] for b in ours]

        def body(it, hs):
            hs = list(hs)
            for i in range(SPAN):
                t = it * SPAN + i
                bb = [bl[at(t * states + v * half, half), :] for v in range(2)]
                for w, b in enumerate(ours):
                    dt = dts[b, pl.ds(t, 1), :]
                    dr = drv[b, pl.ds(t, 1), :]
                    for v in range(2):
                        fade = jnp.exp2(rates[w][v] * dt)
                        hs[2 * w + v] = fade * hs[2 * w + v] + bb[v] * dr
                        hist[b, at(t * states + v * half, half), :] = hs[2 * w + v]
            return tuple(hs)

        zero = jnp.zeros((half, LANES), F32)
        final = lax.fori_loop(0, tokens // SPAN, body, (zero,) * (2 * WAYS))
        for w, b in enumerate(ours):
            for v in range(2):
                tot[b, v * half:(v + 1) * half, :] = final[2 * w + v]

    def sends_end():
        return jnp.logical_or(mine != last, groups > 1)

    def share_ends(q):
        @pl.when(sends_end())
        def _():
            for b in range(q * WAYS, (q + 1) * WAYS):
                spot = SPOTS[b % OWNERS]

                @pl.when(mine != spot)
                def _(b=b, spot=spot):
                    pltpu.make_async_remote_copy(
                        src_ref=tot.at[b], dst_ref=got_e.at[b // OWNERS, mine],
                        send_sem=e_send.at[b // OWNERS], recv_sem=e_recv.at[b // OWNERS, mine],
                        device_id={"seq": base + spot}, device_id_type=MESH).start()

    def weigh(ours):
        entered = [jnp.tile(ent[b].astype(BF16), (SPAN, 1)) for b in ours]
        for g in range(tokens // SPAN):
            here_t = slice(g * SPAN, (g + 1) * SPAN)
            past = slice(g * SPAN * states, (g + 1) * SPAN * states)
            h = jnp.concatenate([gone[b, past, :] * entered[w] for w, b in enumerate(ours)],
                                axis=1)
            y = jnp.dot(cbd[here_t, :], h, preferred_element_type=F32)
            for w, b in enumerate(ours):
                ys[b, here_t, :] = ys[b, here_t, :] + y[:, w * LANES:(w + 1) * LANES]

    def totals(ours):
        line = lax.broadcasted_iota(jnp.int32, (tokens, 2 * tokens), 0)
        lane = lax.broadcasted_iota(jnp.int32, (tokens, 2 * tokens), 1)
        upto = jnp.where(lax.rem(lane, tokens) <= line, 1.0, 0.0).astype(BF16)
        dt = jnp.concatenate([dts[b] for b in ours], axis=1)
        most = dt.astype(BF16)
        rest = (dt - most.astype(F32)).astype(BF16)
        total = jnp.dot(upto, jnp.concatenate([most, rest], axis=0), preferred_element_type=F32)
        for w, b in enumerate(ours):
            dts[b] = total[:, w * LANES:(w + 1) * LANES]

    def fade(ours):
        rates = [rate[b] for b in ours]
        each = OWNERS // len(ours)

        @pl.loop(0, tokens // (SPAN * each))
        def _(it):
            rows = [it * each + e for e in range(each)]
            sums_of = []
            for g in rows:
                past = at(g * (SPAN * states), SPAN * states)
                h = jnp.concatenate([hist[b, past, :].astype(BF16) for b in ours], axis=1)
                sums_of.append(jnp.dot(cbd[at(g * SPAN, SPAN), :], h,
                                       preferred_element_type=F32))
            for i in range(SPAN * each):
                t = it * (SPAN * each) + i
                for w, b in enumerate(ours):
                    gone[b, at(t * states, states), :] = jnp.exp2(
                        rates[w] * dts[b, pl.ds(t, 1), :]).astype(BF16)
            for g, y in zip(rows, sums_of):
                for w, b in enumerate(ours):
                    ys[b, at(g * SPAN, SPAN), :] = y[:, w * LANES:(w + 1) * LANES]

    def drain(part, sem):
        pltpu.make_async_copy(part, part, sem).wait()

    def others(lo, hi, act):
        pl.loop(lo, jnp.clip(mine, lo, hi))(act)
        pl.loop(jnp.clip(mine + 1, lo, hi), hi)(act)

    def holds(ours):
        return jnp.logical_and(is_owner, jnp.logical_and(
            row >= ours[0] % OWNERS, row <= ours[-1] % OWNERS))

    def all_but_own(ref, ours, sem):
        @pl.when(holds(ours))
        def _():
            drain(ref.at[pl.ds(ours[0], len(ours) - 1)], sem)

        @pl.when(jnp.logical_not(holds(ours)))
        def _():
            drain(ref.at[pl.ds(ours[0], len(ours))], sem)

    def own(k, part):
        size = group // 2
        lo, hi = part * size, (part + 1) * size
        block = k * OWNERS + row
        piece = k if k < rounds - 1 else k + row // WAYS

        if k == 0 and part == 0:
            @pl.when(is_owner)
            def _():
                drain(got_s.at[pl.ds(0, group - 1)], s_recv)

        @pl.when(holds(chunks[k]))
        def _():
            rt = rate[block]
            fades = [jnp.exp2(rt * got_s[j, k]) for j in range(max(lo - 1, 0), hi - 1)]
            if part == 0:
                got_e[k, mine] = tot[block]
            if groups == 1:
                others(max(lo - 1, 0), hi - 1, lambda j: drain(got_e.at[k, j], e_recv.at[k, j]))
            carry = jnp.zeros((states, LANES), F32)
            if groups > 1 and part == 0:
                others(0, group, lambda j: drain(got_e.at[k, j], e_recv.at[k, j]))
                end, span = carry, carry
                for j in range(group):
                    end = jnp.exp2(rt * got_s[j, k]) * end + got_e[k, j]
                    span = span + got_s[j, k]
                near[k, 0] = end
                near[k, 1] = span

                @pl.loop(my_group + 1, groups)
                def _(g):
                    pltpu.make_async_remote_copy(
                        src_ref=near.at[k], dst_ref=far.at[k, my_group],
                        send_sem=f_send.at[k, g], recv_sem=f_recv.at[k, my_group],
                        device_id={"seq": g * group + mine}, device_id_type=MESH).start()

                @pl.loop(my_group + 1, groups)
                def _(g):
                    drain(near.at[k], f_send.at[k, g])

                def follow(g, carry):
                    drain(far.at[k, g], f_recv.at[k, g])
                    return jnp.exp2(rt * far[k, g, 1]) * carry + far[k, g, 0]
                carry = lax.fori_loop(0, my_group, follow, carry)
            for j in range(lo, hi):
                if j > 0:
                    before = back[k, j - 1] if j == lo else carry
                    carry = fades[j - 1 - max(lo - 1, 0)] * before + got_e[k, j - 1]
                back[k, j] = carry

            @pl.when(jnp.logical_and(mine >= lo, mine < hi))
            def _():
                ent[block] = back[k, mine]

            def give(j):
                pltpu.make_async_remote_copy(
                    src_ref=back.at[k, j], dst_ref=ent.at[block],
                    send_sem=b_send.at[k], recv_sem=b_recv.at[piece],
                    device_id={"seq": base + j}, device_id_type=MESH).start()
            others(1 if part == 0 and groups == 1 else lo, hi, give)

    def correct(n, ours):
        @pl.when(jnp.logical_or(mine > 0, groups > 1))
        def _():
            all_but_own(ent, ours, b_recv.at[n])
            weigh(ours)

    def finish(ours):
        @pl.loop(ours[0], ours[-1] + 1)
        def _(b):
            cols = columns(b)
            g = g_ref[:, cols].astype(F32)
            mixed = (ys[b] + skip_ref[:, cols] * u_ref[:, cols].astype(F32)) * (
                0.5 * g * (1.0 + jnp.tanh(0.5 * g)))
            out_ref[:, cols] = mixed.astype(out_ref.dtype)

    if blocks % OWNERS:
        for r in range(blocks % OWNERS, OWNERS):
            sums[r, rounds - 1] = jnp.zeros((1, LANES), F32)
    steps()
    spread()
    for q in range(blocks // WAYS):
        ends(q)
        if q == 0:
            meet()
            share_sums()
        share_ends(q)
    place()
    turns = [(k, part) for k in range(rounds) for part in range(2)]
    turns = turns[:1] + [t for i in range(1, len(turns) - 1, 2) for t in (turns[i:i + 2],)] + [
        turns[-1:]]
    turns[0] = [turns[0]]
    for q in range(blocks // WAYS):
        ours = range(q * WAYS, (q + 1) * WAYS)
        totals(ours)
        fade(ours)
        if q < len(turns):
            for k, part in turns[q]:
                own(k, part)
    loads[3].wait()
    loads[4].wait()
    for n, ours in enumerate(pieces):
        correct(n, ours)
        finish(ours)

    @pl.when(is_owner)
    def _():
        drain(sums.at[pl.ds(0, OWNERS - 1)], s_send)

    @pl.when(jnp.logical_not(is_owner))
    def _():
        drain(sums, s_send)
    @pl.when(sends_end())
    def _():
        for k, ours in enumerate(chunks):
            all_but_own(tot, ours, e_send.at[k])
    for k in range(rounds):
        @pl.when(holds(chunks[k]))
        def _(k=k):
            drain(back.at[k, pl.ds(0, group - 1 if groups > 1 else group - 2)], b_send.at[k])


def solution(mesh):
    seq, mp = mesh.shape["seq"], mesh.shape["mp"]

    def per_device(inner_act, gate_act, x_proj, dt_proj, dt_bias, a_log, skip):
        tokens, inner = inner_act.shape
        rank, states = dt_proj.shape[0], a_log.shape[0]
        blocks = inner // LANES
        rounds = pl.cdiv(blocks, OWNERS)
        group = len(SPOTS) * 2
        groups = seq // group
        hbm = pl.BlockSpec(memory_space=pltpu.MemorySpace.HBM)
        args = tuple(pltpu.with_memory_space_constraint(a, pltpu.HBM) for a in (
            inner_act, gate_act, x_proj.T, dt_proj, dt_bias.reshape(1, inner), a_log,
            skip.reshape(1, inner)))
        cell = (states, LANES)
        dma = pltpu.SemaphoreType.DMA
        return pl.pallas_call(
            functools.partial(kernel, seq, mp, tokens, inner, rank, states),
            out_shape=pltpu.VMEM((tokens, inner), jnp.bfloat16),
            in_specs=[hbm] * len(args),
            out_specs=pl.BlockSpec(memory_space=pltpu.VMEM),
            scratch_shapes=[pltpu.VMEM(a.shape, a.dtype) for a in args] + [
                pltpu.VMEM((mp, tokens, x_proj.shape[1]), F32),
                pltpu.VMEM((tokens * states, LANES), F32),
                pltpu.VMEM((tokens, SPAN * states), BF16),
                pltpu.VMEM((blocks,) + cell, F32),
                pltpu.VMEM((blocks, tokens, LANES), F32),
                pltpu.VMEM((blocks, tokens, LANES), F32),
                pltpu.VMEM((blocks, tokens, LANES), F32),
                pltpu.VMEM((blocks, tokens * states, LANES), F32),
                pltpu.VMEM((blocks, tokens * states, LANES), BF16),
                pltpu.VMEM((blocks,) + cell, F32),
                pltpu.VMEM((OWNERS, rounds, 1, LANES), F32),
                pltpu.VMEM((rounds, group) + cell, F32),
                pltpu.VMEM((group, rounds, 1, LANES), F32),
                pltpu.VMEM((rounds, group) + cell, F32),
                pltpu.VMEM((blocks,) + cell, F32),
                pltpu.VMEM((rounds, groups, 2) + cell, F32),
                pltpu.VMEM((rounds, 2) + cell, F32),
                dma((5,)), dma((CUTS, 2)),
                dma((mp - 1,)), dma((mp - 1,)),
                dma((rounds,)), dma((rounds, group)),
                dma, dma,
                dma((rounds,)), dma((rounds + 1,)),
                dma((rounds, groups)), dma((rounds, groups)),
                pltpu.SemaphoreType.REGULAR, pltpu.SemaphoreType.REGULAR,
            ],
            compiler_params=pltpu.CompilerParams(
                collective_id=0, has_side_effects=True,
                vmem_limit_bytes=58 * 1024 * 1024),
        )(*args)

    placed = (
        P("seq", "mp"),
        P("seq", "mp"),
        P("mp", None),
        P(None, "mp"),
        P("mp"),
        P(None, "mp"),
        P("mp"),
    )
    return jax.shard_map(
        per_device, mesh=mesh, in_specs=placed, out_specs=P("seq", "mp"), check_vma=False
    )
```
